32 devices in a mesh: rows: 16 (over z, y, x), cols: 2 (over core).
Axes of the slice: x: 2, y: 2, z: 4, core: 2. Of those that a mesh axis runs over, the one named last changes fastest.
Arguments:
- points: bfloat16 [20480, 512], P('rows', 'cols'), may hold values from -6 to 6
- factor: bfloat16 [20480, 1024], P('rows', 'cols'), may hold values from -2 to 2
- weights: float32 [20480], P('rows'), may hold values from -4 to 4
- pivot_slots: int32 [4, 128], replicated, may hold values from 0 to 1279, as said below
- pivot_owners: int32 [4, 128], replicated, may hold values from 0 to 15
Outputs:
- new_panels: bfloat16 [20480, 512], P('rows', 'cols')
- gram_old: float32 [512, 1024], P('rows', 'cols')
- gram_new: float32 [512, 512], P('rows', 'cols')
The draws below stay inside these ranges and needn't reach their ends.
Inputs may be any that keep to these rules, and one draw needn't show every extreme that they name: Pivot k of panel q is row pivot_slots[q,k] of the block of device pivot_owners[q,k]; the pivots of all panels together are distinct points.
All inputs are finite; a program needn't handle non-finite values.
Results may differ from the reference program's by a relative error of at most 0.009.
Values may be sent and summed in bfloat16 or wider, within the bound.
A program may use at most 64 MiB of HBM per device.

```python
import math
import jax
import jax.numpy as jnp
from jax import lax

F = 512
R = 1024
P_SIZE = 128
PANELS = 4
ROW_DEV = 1280
NPTS = 20480


def pivot_rows_drawn(key):
    order = jax.random.permutation(jax.random.fold_in(key, 29), NPTS)
    picked = order[:PANELS * P_SIZE].astype(jnp.int32).reshape(PANELS, P_SIZE)
    return picked


def draw_pivot_slots(key, part):
    return (pivot_rows_drawn(key) % ROW_DEV).astype(jnp.int32)


def draw_pivot_owners(key, part):
    return (pivot_rows_drawn(key) // ROW_DEV).astype(jnp.int32)


def shard_levels(stream_key, shape, shards, smallest, high):
    loudness, own = 1.0, jax.random.fold_in(stream_key, 6)
    for axis_at, parts in shards:
        draws = jnp.exp(jax.random.uniform(jax.random.fold_in(own, axis_at), (parts,), jnp.float32, smallest / len(shards), high / len(shards)))
        loudness = loudness * jnp.repeat(draws, shape[axis_at] // parts).reshape([-1 if axis == axis_at else 1 for axis in range(len(shape))])
    return loudness


def centred(key, extent, spread, reach, shards=(), held_as=jnp.bfloat16):
    result = spread * jax.random.normal(key, extent, jnp.float32)
    if shards:
        result = result * shard_levels(key, extent, shards, -0.22, 0.18)
    return jnp.clip(result, -reach, reach).astype(held_as)


def setup_inputs(seed: int = 0) -> dict:
    keys = jax.random.split(jax.random.key(seed), 6)
    return {
        "points": centred(keys[0], (NPTS, F), 1.0, 6.0, ((0, 16), (1, 2))),
        "factor": centred(keys[1], (NPTS, R), 0.5, 2.0, ((0, 16), (1, 2))),
        "weights": centred(keys[2], (NPTS,), 1.0, 4.0, ((0, 16),), jnp.float32),
        "pivot_slots": draw_pivot_slots(jax.random.fold_in(keys[5], 71), 0),
        "pivot_owners": draw_pivot_owners(jax.random.fold_in(keys[5], 71), 0),
    }


RIDGE_LEVEL = 1.0

def reference(points, factor, weights, pivot_slots, pivot_owners):
    total = points.shape[0]
    pivot_ids = (pivot_owners * ROW_DEV + pivot_slots).astype(jnp.int32)
    norms = lax.optimization_barrier(jnp.sum(jnp.square(points.astype(jnp.float32)), axis=1))
    built = jnp.zeros((total, PANELS * P_SIZE), jnp.bfloat16)
    row_ids = jnp.arange(total, dtype=jnp.int32)
    identity = jnp.eye(P_SIZE, dtype=jnp.float32)
    for index in range(PANELS):
        chosen = pivot_ids[index]
        sel_points = points[chosen]
        sel_factor = factor[chosen]
        sel_built = built[chosen]
        sel_norms = norms[chosen]
        cross = jnp.dot(points.astype(jnp.float32), sel_points.T.astype(jnp.float32), preferred_element_type=jnp.float32)
        dist = norms[:, None] + sel_norms[None, :] - 2.0 * cross
        schur = jnp.dot(factor.astype(jnp.float32), sel_factor.T.astype(jnp.float32), preferred_element_type=jnp.float32)
        ridge = jnp.where(row_ids[:, None] == chosen[None, :], RIDGE_LEVEL, 0.0).astype(jnp.float32)
        columns = jnp.exp(-dist / F) + ridge + schur / (3.0 * R) - jnp.dot(built.astype(jnp.float32), sel_built.T.astype(jnp.float32), preferred_element_type=jnp.float32)
        block_dist = sel_norms[:, None] + sel_norms[None, :] - 2.0 * jnp.dot(sel_points.astype(jnp.float32), sel_points.T.astype(jnp.float32), preferred_element_type=jnp.float32)
        block = jnp.exp(-block_dist / F) + RIDGE_LEVEL * identity + jnp.dot(sel_factor.astype(jnp.float32), sel_factor.T.astype(jnp.float32), preferred_element_type=jnp.float32) / (3.0 * R) - jnp.dot(sel_built.astype(jnp.float32), sel_built.T.astype(jnp.float32), preferred_element_type=jnp.float32)
        lower = jnp.linalg.cholesky(block)
        inverse = lax.linalg.triangular_solve(lower, identity, left_side=True, lower=True)
        fresh = jnp.dot(columns, inverse.T, precision=lax.Precision.HIGHEST).astype(jnp.bfloat16)
        built = built.at[:, index * P_SIZE:(index + 1) * P_SIZE].set(fresh)
    weighted = (built.astype(jnp.float32) * weights[:, None]).astype(jnp.bfloat16)
    dims = (((0,), (0,)), ((), ()))
    scale = P_SIZE / math.sqrt(total)
    gram_old = lax.dot_general(weighted.astype(jnp.float32), factor.astype(jnp.float32), dims, preferred_element_type=jnp.float32) * scale
    gram_new = lax.dot_general(weighted.astype(jnp.float32), built.astype(jnp.float32), dims, preferred_element_type=jnp.float32) * scale
    return (built, gram_old, gram_new)
```

```python
import functools
import math

import jax
import jax.numpy as jnp
from jax import lax
from jax.experimental import pallas as pl
from jax.experimental.pallas import tpu as pltpu
from jax.sharding import PartitionSpec as P

RIDGE_LEVEL = 1.0
BLOCK = 8
VMEM = pltpu.VMEM
HIGH = lax.Precision.HIGHEST
NT = (((1,), (1,)), ((), ()))
TN = (((0,), (0,)), ((), ()))


def remote(src, dst, send, recv, row, col):
    return pltpu.make_async_remote_copy(
        src_ref=src, dst_ref=dst, send_sem=send, recv_sem=recv,
        device_id=(row, col), device_id_type=pl.DeviceIdType.MESH,
    )


def peers_of(me, col, inner, outer):
    place, layer = me % inner, me // inner
    peers = [(me, 1 - col)]
    peers += [(layer * inner + (place + d) % inner, col) for d in range(1, inner)]
    peers += [(((layer + d) % outer) * inner + place, col) for d in range(1, outer)]
    return peers


def factor_block(size, a, e, rows, wide, hooks):
    for first in range(0, size, BLOCK):
        if first in hooks:
            hooks[first]()
        span = slice(first, first + BLOCK)
        strip = a[span, :]
        for k in range(BLOCK):
            wide[first // BLOCK % 2 * BLOCK + k] = jnp.broadcast_to(strip[:, first + k:first + k + 1], (BLOCK, size))
        d = {(i, k): wide[first // BLOCK % 2 * BLOCK + k, i:i + 1, :] for i in range(BLOCK) for k in range(i + 1)}
        r = [a[first + i:first + i + 1, :] for i in range(BLOCK)]
        s = [e[first + i:first + i + 1, :] for i in range(BLOCK)]
        for k in range(BLOCK):
            scale = lax.rsqrt(d[k, k])
            r[k] = r[k] * scale
            s[k] = s[k] * scale
            for i in range(k + 1, BLOCK):
                d[i, k] = d[i, k] * scale
            for i in range(k + 1, BLOCK):
                r[i] = r[i] - d[i, k] * r[k]
                s[i] = s[i] - d[i, k] * s[k]
                for m in range(k + 1, i + 1):
                    d[i, m] = d[i, m] - d[i, k] * d[m, k]
        base = BLOCK * (first // BLOCK % 2)
        for k in range(BLOCK):
            rows[base + k:base + k + 1, :] = r[k]
            e[first + k:first + k + 1, :] = s[k]
        after = first + BLOCK
        if after < size:
            upper = jnp.transpose(rows[base:base + BLOCK, :])
            for low, high in ((after, after + BLOCK), (after + BLOCK, size)):
                if low < high:
                    rest_a = a[low:high, :]
                    rest_e = e[low:high, :]
                    for k in range(BLOCK):
                        column = upper[low:high, k:k + 1]
                        rest_a = rest_a - column * rows[base + k:base + k + 1, :]
                        rest_e = rest_e - column * e[first + k:first + k + 1, :]
                    a[low:high, :] = rest_a
                    e[low:high, :] = rest_e


def panel_kernel(inner, outer, scale_by, slots, owners, points_in, factor_in, weights, own_cols, gram_old, gram_new,
                 out_ref, other_ref, level_t, gp, ga, gacc, gmid, gb, nw, na, nacc, nmid, nb,
                 ga_send, ga_recv, gb_send, gb_recv, na_send, na_recv, nb_send, nb_recv,
                 points, factor, load, part, piv, other_points, other_factor, buf_a, buf_b, acc,
                 prow, inv, norms, a, early, ready, columns, rows, wide,
                 a_send, a_recv, b_send, b_recv, f_send, f_recv,
                 d_send, d_recv, e_send, e_recv, x_send, x_recv):
    me = lax.axis_index("rows")
    col = lax.axis_index("cols")
    place, layer = me % inner, me // inner
    panels, size = slots.shape
    here, fw = points.shape
    half = here // 2
    feats, rank = 2 * fw, 2 * factor.shape[1]
    chunk = size // inner
    f32, bf16 = jnp.float32, jnp.bfloat16

    loads = [
        pltpu.make_async_copy(points_in, points, load.at[0]),
        pltpu.make_async_copy(factor_in, factor, load.at[1]),
    ]
    for c in loads:
        c.start()
    barrier = pltpu.get_barrier_semaphore()
    peers = peers_of(me, col, inner, outer)
    for peer in peers:
        pl.semaphore_signal(barrier, inc=1, device_id=peer, device_id_type=pl.DeviceIdType.MESH)

    def piece(q, p):
        return pl.ds(pl.multiple_of(q * size + p * chunk, chunk), chunk)

    def turned(row):
        return jnp.transpose(jnp.broadcast_to(row, (size, size)))

    spots = lax.broadcasted_iota(jnp.int32, (size, here), 1) + me * here

    def gather(q):
        ids = (owners[q:q + 1, :] * here + slots[q:q + 1, :]).astype(f32)
        hot = jnp.where(spots == turned(ids)[:, 0:1].astype(jnp.int32), 1.0, 0.0).astype(bf16)
        span = slice(q * size, (q + 1) * size)
        part[span, :fw] = jnp.dot(hot, points[...], preferred_element_type=f32).astype(bf16)
        part[span, fw:] = jnp.dot(hot, factor[...], preferred_element_type=f32).astype(bf16)

    def within(q, d):
        p = (place + d) % inner
        return remote(part.at[piece(q, p)], buf_a.at[q, d - 1], a_send.at[q, d - 1], a_recv.at[q, d - 1],
                      layer * inner + p, col)

    def along(q, d):
        return remote(acc.at[q], buf_b.at[q, d - 1], b_send.at[q, d - 1], b_recv.at[q, d - 1],
                      ((layer + d) % outer) * inner + place, col)

    def around(q, d):
        it = piv.at[col, piece(q, place)]
        return remote(it, it, d_send.at[q, d - 1], d_recv.at[q, d - 1], layer * inner + (place + d) % inner, col)

    def across(q, d):
        it = piv.at[col, piece(q, (place + inner - d) % inner)]
        return remote(it, it, e_send.at[q, d], e_recv.at[q, d], me, 1 - col)

    def swap_panel(q):
        span = slice(q * size, (q + 1) * size)
        return remote(out_ref.at[:, span], other_ref.at[:, span], f_send.at[q], f_recv.at[q], me, 1 - col)

    def layer_start(q):
        for d in range(1, inner):
            within(q, d).start()

    def layer_sum(q):
        total = part[piece(q, place), :]
        for d in range(1, inner):
            within(q, d).wait_recv()
            total = total + buf_a[q, d - 1]
        acc[q] = total
        for d in range(1, outer):
            along(q, d).start()

    def whole_sum(q):
        total = acc[q]
        for d in range(1, outer):
            along(q, d).wait_recv()
            total = total + buf_b[q, d - 1]
        piv[col, piece(q, place)] = total
        for d in range(1, inner):
            around(q, d).start()
        across(q, 0).start()

    def forward(q):
        for d in range(1, inner):
            around(q, d).wait_recv()
            across(q, d).start()

    def arrive(q):
        for d in range(inner):
            across(q, d).wait_recv()

    theirs = pl.ds(pl.multiple_of((1 - col) * half, 16), half)
    swap = [
        remote(points.at[theirs], other_points, x_send.at[0], x_recv.at[0], me, 1 - col),
        remote(factor.at[theirs], other_factor, x_send.at[1], x_recv.at[1], me, 1 - col),
    ]

    for c in loads:
        c.wait()
    gather(0)
    pl.semaphore_wait(barrier, len(peers))
    layer_start(0)
    for c in swap:
        c.start()
    for q in range(1, panels):
        gather(q)
    layer_sum(0)
    if panels > 1:
        layer_start(1)

    def norm(x, y):
        x, y = x.astype(f32), y.astype(f32)
        return jnp.sum(x * x, axis=1, keepdims=True) + jnp.sum(y * y, axis=1, keepdims=True)

    def dot(x, y):
        return lax.dot_general(x, y, NT, preferred_element_type=f32)

    def exact(x, y):
        return lax.dot_general(x, y, NT, precision=HIGH, preferred_element_type=f32)

    for c in swap:
        c.wait_recv()
    mine = pl.ds(pl.multiple_of(col * half, 16), half)
    own_norm = norm(points[mine, :], other_points[...])
    own_ids = lax.broadcasted_iota(jnp.int32, (half, size), 0) + (me * here + col * half)
    same = lax.broadcasted_iota(jnp.int32, (size, size), 0) == lax.broadcasted_iota(jnp.int32, (size, size), 1)
    eye = jnp.where(same, 1.0, 0.0)

    whole_sum(0)
    if panels > 1:
        layer_sum(1)
    if panels > 2:
        layer_start(2)
    forward(0)

    runs = gp.shape[1]
    lines = gp.shape[3]
    width = own_cols.shape[1]
    wide_lanes = pl.ds(pl.multiple_of(col * width, 128), width)

    def gram_a(k, d):
        p = (place + d) % inner
        return remote(gp.at[k, :, p], ga.at[k, d - 1], ga_send.at[k, d - 1], ga_recv.at[k, d - 1],
                      layer * inner + p, col)

    def gram_b(k, i):
        target = k * runs + i
        slot = (layer - target + 2 * outer - 1) % outer
        return remote(gmid.at[k, i], gb.at[slot], gb_send.at[k, i], gb_recv.at[slot], target * inner + place, col)

    def gram_got(d):
        return remote(gmid.at[0, 0], gb.at[d - 1], gb_send.at[0, 0], gb_recv.at[d - 1],
                      ((layer + d) % outer) * inner + place, col)

    def new_a(d):
        p = (place + d) % inner
        return remote(nw.at[:, p], na.at[d - 1], na_send.at[d - 1], na_recv.at[d - 1], layer * inner + p, col)

    def new_b(d):
        z = (layer + d) % outer
        return remote(nmid.at[z], nb.at[d - 1], nb_send.at[d - 1], nb_recv.at[d - 1], z * inner + place, col)

    def gram_block(k):
        swap_panel(k).wait_recv()
        lanes = slice(k * size, (k + 1) * size)
        for source, which in ((out_ref, col), (other_ref, 1 - col)):
            for i in range(half // size):
                level = turned(weights[pl.ds(which * (half // size) + i, 1), :])[:, 0:1]
                block = source[i * size:(i + 1) * size, lanes].astype(f32) * level
                first = pl.multiple_of(which * half + i * size, size)
                level_t[lanes, pl.ds(first, size)] = jnp.transpose(block).astype(bf16)
        block = jnp.dot(level_t[lanes, :], factor[...], preferred_element_type=f32) * scale_by
        gp[k] = block.reshape(runs, inner, lines, factor.shape[1]).astype(bf16)
        for d in range(1, inner):
            gram_a(k, d).start()

    def gram_sum(k):
        total = gp[k, :, place].astype(f32)
        for d in range(1, inner):
            gram_a(k, d).wait_recv()
            total = total + ga[k, d - 1].astype(f32)
        gacc[k] = total
        gmid[k] = total.astype(bf16)
        for i in range(runs):
            @pl.when(layer != k * runs + i)
            def _():
                gram_b(k, i).start()

    def span(q):
        return slice(q * size, (q + 1) * size)

    def entries(xs, xo, ys, yo, q, row_norms):
        ts, to = piv[col, span(q), :], piv[1 - col, span(q), :]
        cross = dot(xs, ts[:, :fw]) + dot(xo, to[:, :fw])
        schur = dot(ys, ts[:, fw:]) + dot(yo, to[:, fw:])
        return jnp.exp(-(row_norms + norms[q, 0:1, :] - 2.0 * cross) / feats) + schur / (3.0 * rank)

    def less(value, x, y, count):
        if count:
            return value - dot(x[:, :count * size], y[:, :count * size])
        return value

    def head(r):
        ps, po = piv[col, span(r), :], piv[1 - col, span(r), :]
        pnorm = norm(ps[:, :fw], po[:, :fw])
        norms[r] = jnp.transpose(jnp.broadcast_to(pnorm, (size, size)))

        def against(k):
            return entries(ps[:, :fw], po[:, :fw], ps[:, fw:], po[:, fw:], k, pnorm)

        for k in range(r):
            m = less(against(k), prow[r], prow[k], k)
            if k < r - 1:
                prow[r, :, span(k)] = exact(m, inv[k]).astype(bf16)
            else:
                ready[...] = m
        early[...] = less(against(r) + RIDGE_LEVEL * eye, prow[r], prow[r], max(r - 1, 0))

    def begin(r):
        if r:
            fresh = exact(ready[...], inv[r - 1]).astype(bf16)
            prow[r, :, span(r - 1)] = fresh
            a[...] = early[...] - dot(fresh, fresh)
        else:
            a[...] = early[...]
        inv[r] = eye

    def solve(r):
        out_ref[:, span(r)] = exact(columns[...], inv[r]).astype(bf16)

    def fill(r):
        ids = owners[r:r + 1, :] * here + slots[r:r + 1, :]
        value = entries(points[mine, :], other_points[...], factor[mine, :], other_factor[...], r, own_norm)
        value = value + jnp.where(own_ids == ids, RIDGE_LEVEL, 0.0)
        columns[...] = less(value, out_ref, prow[r], r)

    arrive(0)
    head(0)
    for q in range(panels):
        def first_hook():
            if q == 0 and panels > 1:
                whole_sum(1)
                if panels > 2:
                    layer_sum(2)
                if panels > 3:
                    layer_start(3)
            if q > 0:
                swap_panel(q - 1).start()
            if q > 0 and q + 1 < panels:
                forward(q + 1)

        def second_hook():
            if q == 0 and panels > 1:
                forward(1)
            if q + 2 < panels:
                whole_sum(q + 2)
            if q + 3 < panels:
                layer_sum(q + 3)
            if q > 0:
                gram_block(q - 1)
            if q > 1:
                gram_sum(q - 2)
            if q > 0 and q + 1 < panels:
                arrive(q + 1)
                head(q + 1)

        def third_hook():
            if q == 0 and panels > 1:
                arrive(1)
                head(1)

        begin(q)
        if q:
            solve(q - 1)
        fill(q)
        factor_block(size, a, inv.at[q], rows, wide, {4 * BLOCK: first_hook, 10 * BLOCK: second_hook, 14 * BLOCK: third_hook})
    solve(panels - 1)
    swap_panel(panels - 1).start()
    if panels > 1:
        gram_sum(panels - 2)
    gram_block(panels - 1)
    for source, which in ((out_ref, col), (other_ref, 1 - col)):
        own_cols[pl.ds(pl.multiple_of(which * half, 16), half), :] = source[:, wide_lanes]
    block = jnp.dot(level_t[...], own_cols[...], preferred_element_type=f32) * scale_by
    nw[...] = block.reshape(outer, inner, lines, width).astype(bf16)
    for d in range(1, inner):
        new_a(d).start()
    gram_sum(panels - 1)
    total = nw[:, place].astype(f32)
    for d in range(1, inner):
        new_a(d).wait_recv()
        total = total + na[d - 1].astype(f32)
    nacc[...] = total
    nmid[...] = total.astype(bf16)
    for d in range(1, outer):
        new_b(d).start()
    total = gacc[layer // runs, layer % runs]
    for d in range(1, outer):
        gram_got(d).wait_recv()
        total = total + gb[d - 1].astype(f32)
    gram_old[...] = total
    total = nacc[layer]
    for d in range(1, outer):
        new_b(d).wait_recv()
        total = total + nb[d - 1].astype(f32)
    gram_new[...] = total
    for d in range(1, inner):
        new_a(d).wait_send()
    for d in range(1, outer):
        new_b(d).wait_send()
    for c in swap:
        c.wait_send()
    for q in range(panels):
        swap_panel(q).wait_send()
        for d in range(1, inner):
            within(q, d).wait_send()
            gram_a(q, d).wait_send()
        for i in range(runs):
            @pl.when(layer != q * runs + i)
            def _():
                gram_b(q, i).wait_send()
        for d in range(1, outer):
            along(q, d).wait_send()
        for d in range(1, inner):
            around(q, d).wait_send()
        for d in range(inner):
            across(q, d).wait_send()


def write_kernel(a, b, c, x, y, z, sems):
    copies = [pltpu.make_async_copy(s, d, sems.at[i]) for i, (s, d) in enumerate(((a, x), (b, y), (c, z)))]
    for c in copies:
        c.start()
    for c in copies:
        c.wait()


def body(points, factor, weights, pivot_slots, pivot_owners):
    here, fw = points.shape
    rank = factor.shape[1]
    panels, size = pivot_slots.shape
    rows = lax.axis_size("rows")
    count = panels * size
    chunk = count // rows
    width = fw + rank
    half = here // 2
    bf16, f32 = jnp.bfloat16, jnp.float32
    vm = pl.BlockSpec(memory_space=VMEM)
    hbm = pl.BlockSpec(memory_space=pl.ANY)
    sem = lambda *n: pltpu.SemaphoreType.DMA(n)
    limit = 60 * 1024 * 1024

    split = rows // panels if rows < panels * panels else panels
    layers = rows // split
    piece = size // split
    runs = layers // panels
    share = count // 2
    scale = size / math.sqrt(here * rows)
    outs = pl.pallas_call(
        functools.partial(panel_kernel, split, layers, scale),
        out_shape=(
            pltpu.VMEM((here, share), bf16), pltpu.VMEM((chunk, rank), f32), pltpu.VMEM((chunk, share), f32),
        ),
        in_specs=[vm, vm, hbm, hbm, vm], out_specs=(vm,) * 3, name="panels",
        scratch_shapes=[
            VMEM((half, count), bf16), VMEM((half, count), bf16), VMEM((count, here), bf16),
            VMEM((panels, runs, split, chunk, rank), bf16),
            VMEM((panels, split - 1, runs, chunk, rank), bf16),
            VMEM((panels, runs, chunk, rank), f32), VMEM((panels, runs, chunk, rank), bf16),
            VMEM((layers, chunk, rank), bf16),
            VMEM((layers, split, chunk, share), bf16),
            VMEM((split - 1, layers, chunk, share), bf16),
            VMEM((layers, chunk, share), f32), VMEM((layers, chunk, share), bf16),
            VMEM((layers - 1, chunk, share), bf16),
            sem(panels, split - 1), sem(panels, split - 1), sem(panels, runs), sem(layers),
            sem(split - 1), sem(split - 1), sem(layers - 1), sem(layers - 1),
            VMEM((here, fw), bf16), VMEM((here, rank), bf16), sem(2),
            VMEM((count, width), bf16), VMEM((2, count, width), bf16),
            VMEM((half, fw), bf16), VMEM((half, rank), bf16),
            VMEM((panels, split - 1, piece, width), bf16),
            VMEM((panels, layers - 1, piece, width), bf16),
            VMEM((panels, piece, width), bf16),
            VMEM((panels, size, count), bf16),
            VMEM((panels, size, size), f32), VMEM((panels, size, size), f32), VMEM((size, size), f32),
            VMEM((size, size), f32), VMEM((size, size), f32), VMEM((half, size), f32),
            VMEM((2 * BLOCK, size), f32), VMEM((2 * BLOCK, BLOCK, size), f32),
            sem(panels, split - 1), sem(panels, split - 1), sem(panels, layers - 1), sem(panels, layers - 1),
            sem(panels), sem(panels), sem(panels, split - 1), sem(panels, split - 1),
            sem(panels, split), sem(panels, split), sem(2), sem(2),
        ],
        compiler_params=pltpu.CompilerParams(collective_id=0, has_side_effects=True, vmem_limit_bytes=limit),
    )(pivot_slots, pivot_owners, points, factor, weights.reshape(here // size, size))
    return pl.pallas_call(
        write_kernel,
        out_shape=(
            jax.ShapeDtypeStruct((here, share), bf16),
            jax.ShapeDtypeStruct((chunk, rank), f32),
            jax.ShapeDtypeStruct((chunk, share), f32),
        ),
        in_specs=[vm] * 3, out_specs=(hbm,) * 3, name="write",
        scratch_shapes=[sem(3)],
    )(*[pltpu.with_memory_space_constraint(v, pltpu.VMEM) for v in outs])


def solution(mesh):
    return jax.shard_map(
        body,
        mesh=mesh,
        in_specs=(P("rows", "cols"), P("rows", "cols"), P("rows"), P(), P()),
        out_specs=(P("rows", "cols"), P("rows", "cols"), P("rows", "cols")),
        check_vma=False,
    )
```

```python
import functools
import math

import jax
import jax.numpy as jnp
from jax import lax
from jax.experimental import pallas as pl
from jax.experimental.pallas import tpu as pltpu
from jax.sharding import PartitionSpec as P

RIDGE_LEVEL = 1.0
BLOCK = 8
HOOKS = (4, 8, 12, 14)
VMEM = pltpu.VMEM
HIGH = lax.Precision.HIGHEST
NT = (((1,), (1,)), ((), ()))
TN = (((0,), (0,)), ((), ()))


def remote(src, dst, send, recv, row, col):
    return pltpu.make_async_remote_copy(
        src_ref=src, dst_ref=dst, send_sem=send, recv_sem=recv,
        device_id=(row, col), device_id_type=pl.DeviceIdType.MESH,
    )


def peers_of(me, col, inner, outer):
    place, layer = me % inner, me // inner
    peers = [(me, 1 - col)]
    peers += [(layer * inner + (place + d) % inner, col) for d in range(1, inner)]
    peers += [(((layer + d) % outer) * inner + place, col) for d in range(1, outer)]
    return peers


def pivot_chain(d):
    scales = []
    for k in range(0, BLOCK, 2):
        first = lax.rsqrt(d[k, k])
        both = lax.rsqrt(d[k, k] * d[k + 1, k + 1] - d[k + 1, k] * d[k + 1, k])
        scales += [first, both * (d[k, k] * first)]
        step = both * first
        for i in range(k + 2, BLOCK):
            d[i, k + 1] = (d[k, k] * d[i, k + 1] - d[i, k] * d[k + 1, k]) * step
        for i in range(k + 1, BLOCK):
            d[i, k] = d[i, k] * first
        for i in range(k + 2, BLOCK):
            for m in range(k + 2, i + 1):
                d[i, m] = d[i, m] - d[i, k] * d[m, k] - d[i, k + 1] * d[m, k + 1]
    return scales


def solve_rows(d, scales, z):
    for k in range(BLOCK):
        z[k] = z[k] * scales[k]
        for i in range(k + 1, BLOCK):
            z[i] = z[i] - d[i, k] * z[k]
    return z


def factor_block(size, x, rows, wide, hooks):
    deep = 2 * BLOCK
    lane = lax.broadcasted_iota(jnp.int32, (BLOCK, size), 1)
    line = lax.broadcasted_iota(jnp.int32, (BLOCK, size), 0)

    def full(ref, i):
        return jnp.broadcast_to(ref[i:i + 1, :], (BLOCK, size))

    for first in range(0, size, deep):
        if first in hooks:
            hooks[first]()
        turn = first // deep % 2
        base, at = 3 * BLOCK * turn, deep * turn
        middle, after = first + BLOCK, first + deep
        inside = (lane >= first) & (lane < after)
        top = x[first:middle, :]
        low = x[middle:after, :]
        for k in range(BLOCK):
            for slot, part, spot in ((0, top, first + k), (1, low, first + k), (2, low, middle + k)):
                wide[base + slot * BLOCK + k] = jnp.broadcast_to(part[:, spot:spot + 1], (BLOCK, size))
        d = {(i, k): full(wide.at[base + k], i) for i in range(BLOCK) for k in range(i + 1)}
        scales = pivot_chain(d)
        left = []
        for k in range(BLOCK):
            w = wide[base + BLOCK + k]
            for m in range(k):
                w = w - d[k, m] * left[m]
            left.append(w * scales[k])
            wide[base + BLOCK + k] = left[k]
        z = [jnp.where(inside, jnp.where(lane == first + i, 1.0, 0.0), full(x, first + i)) for i in range(BLOCK)]
        z = solve_rows(d, scales, z)
        under = jnp.where(inside, jnp.where(lane == middle + line, 1.0, 0.0), low)
        for k in range(BLOCK):
            under = under - left[k] * z[k]
            rows[at + k:at + k + 1, :] = z[k][0:1, :]
        x[middle:after, :] = under
        for m in range(BLOCK):
            v = wide[base + 2 * BLOCK + m]
            for k in range(BLOCK):
                v = v - left[k] * full(wide.at[base + BLOCK + k], m)
            wide[base + 2 * BLOCK + m] = v
        d = {(i, k): full(wide.at[base + 2 * BLOCK + k], i) for i in range(BLOCK) for k in range(i + 1)}
        scales = pivot_chain(d)
        z = solve_rows(d, scales, [full(x, middle + i) for i in range(BLOCK)])
        for k in range(BLOCK):
            rows[at + BLOCK + k:at + BLOCK + k + 1, :] = z[k][0:1, :]
        done = rows[at:at + deep, :]
        x[first:after, :] = jnp.where(lax.broadcasted_iota(jnp.int32, (deep, size), 1) < after, done, 0.0)
        if after < size:
            upper = jnp.transpose(done)
            for start, stop in ((after, after + deep), (after + deep, size)):
                if start < stop:
                    spots = lax.broadcasted_iota(jnp.int32, (stop - start, size), 1)
                    rest = jnp.where((spots >= first) & (spots < after), 0.0, x[start:stop, :])
                    for k in range(deep):
                        rest = rest - upper[start:stop, k:k + 1] * rows[at + k:at + k + 1, :]
                    x[start:stop, :] = rest


def panel_kernel(inner, outer, scale_by, slots, owners, points_in, factor_in, weights, own_cols, gram_old, gram_new,
                 out_ref, other_ref, level_t, gp, ga, gacc, gmid, gb, nw, na, nacc, nmid, nb,
                 cw, ca, cacc, cmid, cb,
                 ga_send, ga_recv, gb_send, gb_recv, na_send, na_recv, nb_send, nb_recv,
                 ca_send, ca_recv, cb_send, cb_recv,
                 points, factor, load, part, piv, other_points, other_factor, buf_a, buf_b, acc,
                 prow, inv, norms, early, ready, columns, rows, wide,
                 a_send, a_recv, b_send, b_recv, f_send, f_recv,
                 d_send, d_recv, e_send, e_recv, x_send, x_recv):
    me = lax.axis_index("rows")
    col = lax.axis_index("cols")
    place, layer = me % inner, me // inner
    panels, size = slots.shape
    here, fw = points.shape
    half = here // 2
    feats, rank = 2 * fw, 2 * factor.shape[1]
    chunk = size // inner
    f32, bf16 = jnp.float32, jnp.bfloat16

    loads = [
        pltpu.make_async_copy(points_in, points, load.at[0]),
        pltpu.make_async_copy(factor_in, factor, load.at[1]),
    ]
    for c in loads:
        c.start()
    barrier = pltpu.get_barrier_semaphore()
    peers = peers_of(me, col, inner, outer)
    for peer in peers:
        pl.semaphore_signal(barrier, inc=1, device_id=peer, device_id_type=pl.DeviceIdType.MESH)

    def piece(q, p):
        return pl.ds(pl.multiple_of(q * size + p * chunk, chunk), chunk)

    def turned(row):
        return jnp.transpose(jnp.broadcast_to(row, (size, size)))

    spots = lax.broadcasted_iota(jnp.int32, (size, here), 1) + me * here

    def gather(q):
        ids = (owners[q:q + 1, :] * here + slots[q:q + 1, :]).astype(f32)
        hot = jnp.where(spots == turned(ids)[:, 0:1].astype(jnp.int32), 1.0, 0.0).astype(bf16)
        span = slice(q * size, (q + 1) * size)
        part[span, :fw] = jnp.dot(hot, points[...], preferred_element_type=f32).astype(bf16)
        part[span, fw:] = jnp.dot(hot, factor[...], preferred_element_type=f32).astype(bf16)

    def within(q, d):
        p = (place + d) % inner
        return remote(part.at[piece(q, p)], buf_a.at[q, d - 1], a_send.at[q, d - 1], a_recv.at[q, d - 1],
                      layer * inner + p, col)

    def along(q, d):
        return remote(acc.at[q], buf_b.at[q, d - 1], b_send.at[q, d - 1], b_recv.at[q, d - 1],
                      ((layer + d) % outer) * inner + place, col)

    def around(q, d):
        it = piv.at[col, piece(q, place)]
        return remote(it, it, d_send.at[q, d - 1], d_recv.at[q, d - 1], layer * inner + (place + d) % inner, col)

    def across(q, d):
        it = piv.at[col, piece(q, (place + inner - d) % inner)]
        return remote(it, it, e_send.at[q, d], e_recv.at[q, d], me, 1 - col)

    def swap_panel(q):
        span = slice(q * size, (q + 1) * size)
        return remote(out_ref.at[:, span], other_ref.at[:, span], f_send.at[q], f_recv.at[q], me, 1 - col)

    def layer_start(q):
        for d in range(1, inner):
            within(q, d).start()

    def layer_sum(q):
        total = part[piece(q, place), :]
        for d in range(1, inner):
            within(q, d).wait_recv()
            total = total + buf_a[q, d - 1]
        acc[q] = total
        for d in range(1, outer):
            along(q, d).start()

    def whole_sum(q):
        total = acc[q]
        for d in range(1, outer):
            along(q, d).wait_recv()
            total = total + buf_b[q, d - 1]
        piv[col, piece(q, place)] = total
        for d in range(1, inner):
            around(q, d).start()
        across(q, 0).start()

    def forward(q):
        for d in range(1, inner):
            around(q, d).wait_recv()
            across(q, d).start()

    def arrive(q):
        for d in range(inner):
            across(q, d).wait_recv()

    theirs = pl.ds(pl.multiple_of((1 - col) * half, 16), half)
    swap = [
        remote(points.at[theirs], other_points, x_send.at[0], x_recv.at[0], me, 1 - col),
        remote(factor.at[theirs], other_factor, x_send.at[1], x_recv.at[1], me, 1 - col),
    ]

    for c in loads:
        c.wait()
    gather(0)
    pl.semaphore_wait(barrier, len(peers))
    layer_start(0)
    for c in swap:
        c.start()
    for q in range(1, panels):
        gather(q)
        if q == 1:
            layer_start(1)
    layer_sum(0)
    if panels > 1:
        layer_sum(1)
    if panels > 2:
        layer_start(2)

    def norm(x, y):
        x, y = x.astype(f32), y.astype(f32)
        return jnp.sum(x * x, axis=1, keepdims=True) + jnp.sum(y * y, axis=1, keepdims=True)

    def dot(x, y):
        return lax.dot_general(x, y, NT, preferred_element_type=f32)

    def exact(x, y):
        return lax.dot_general(x, y, NT, precision=HIGH, preferred_element_type=f32)

    for c in swap:
        c.wait_recv()
    mine = pl.ds(pl.multiple_of(col * half, 16), half)
    own_norm = norm(points[mine, :], other_points[...])
    own_ids = lax.broadcasted_iota(jnp.int32, (half, size), 0) + (me * here + col * half)
    same = lax.broadcasted_iota(jnp.int32, (size, size), 0) == lax.broadcasted_iota(jnp.int32, (size, size), 1)
    eye = jnp.where(same, 1.0, 0.0)

    if panels > 2:
        layer_sum(2)
    whole_sum(0)
    if panels > 3:
        layer_start(3)
    forward(0)
    if panels > 1:
        whole_sum(1)

    runs = gp.shape[1]
    lines = gp.shape[3]
    width = own_cols.shape[1]

    def gram_a(k, d):
        p = (place + d) % inner
        return remote(gp.at[k, :, p], ga.at[k, d - 1], ga_send.at[k, d - 1], ga_recv.at[k, d - 1],
                      layer * inner + p, col)

    def gram_b(k, i):
        target = k * runs + i
        slot = (layer - target + 2 * outer - 1) % outer
        return remote(gmid.at[k, i], gb.at[slot], gb_send.at[k, i], gb_recv.at[slot], target * inner + place, col)

    def gram_got(d):
        return remote(gmid.at[0, 0], gb.at[d - 1], gb_send.at[0, 0], gb_recv.at[d - 1],
                      ((layer + d) % outer) * inner + place, col)

    cut = outer - runs
    count = panels * size

    def half_rows(which):
        return pl.ds(pl.multiple_of(which * half, 16), half)

    def slot_of(z):
        return (layer - z + 2 * outer - 1) % outer

    def new_a(late, d):
        p = (place + d) % inner
        rows_of = slice(cut, outer) if late else slice(0, cut)
        return remote(nw.at[rows_of, p], na.at[d - 1, rows_of], na_send.at[late, d - 1], na_recv.at[late, d - 1],
                      layer * inner + p, col)

    def new_b(z):
        return remote(nmid.at[z], nb.at[slot_of(z)], nb_send.at[z], nb_recv.at[slot_of(z)], z * inner + place, col)

    def new_got(d):
        return remote(nmid.at[0], nb.at[d - 1], nb_send.at[0], nb_recv.at[d - 1],
                      ((layer + d) % outer) * inner + place, col)

    def side_a(d):
        p = (place + d) % inner
        return remote(cw.at[:, p], ca.at[d - 1], ca_send.at[d - 1], ca_recv.at[d - 1], layer * inner + p, col)

    def side_b(z):
        return remote(cmid.at[z], cb.at[slot_of(z)], cb_send.at[z], cb_recv.at[slot_of(z)], z * inner + place, col)

    def side_got(d):
        return remote(cmid.at[0], cb.at[d - 1], cb_send.at[0], cb_recv.at[d - 1],
                      ((layer + d) % outer) * inner + place, col)

    def new_early():
        for source, which in ((out_ref, col), (other_ref, 1 - col)):
            own_cols[half_rows(which), :width - size] = source[:, pl.ds(pl.multiple_of(col * width, 128), width - size)]

        @pl.when(col == 0)
        def _():
            for source, which in ((out_ref, col), (other_ref, 1 - col)):
                own_cols[half_rows(which), width - size:] = source[:, width - size:width]

        @pl.when(col == 1)
        def _():
            own_cols[:, width - size:] = jnp.zeros((here, size), bf16)

        block = jnp.dot(level_t[:count - size, :], own_cols[...], preferred_element_type=f32) * scale_by
        nw[:cut] = block.reshape(cut, inner, lines, width).astype(bf16)

    def new_sum(late):
        rows_of = slice(cut, outer) if late else slice(0, cut)
        total = nw[rows_of, place].astype(f32)
        for d in range(1, inner):
            new_a(late, d).wait_recv()
            total = total + na[d - 1, rows_of].astype(f32)
        nacc[rows_of] = total
        nmid[rows_of] = total.astype(bf16)
        for z in range(outer)[rows_of]:
            @pl.when(layer != z)
            def _():
                new_b(z).start()

    def gram_block(k):
        lanes = slice(k * size, (k + 1) * size)

        def part_of(source, which):
            for i in range(half // size):
                level = turned(weights[pl.ds(which * (half // size) + i, 1), :])[:, 0:1]
                block = source[i * size:(i + 1) * size, lanes].astype(f32) * level
                first = pl.multiple_of(which * half + i * size, size)
                level_t[lanes, pl.ds(first, size)] = jnp.transpose(block).astype(bf16)
            spots = pl.ds(pl.multiple_of(which * half, size), half)
            return jnp.dot(level_t[lanes, spots], factor[half_rows(which), :], preferred_element_type=f32)

        block = part_of(out_ref, col)
        swap_panel(k).wait_recv()
        block = (block + part_of(other_ref, 1 - col)) * scale_by
        gp[k] = block.reshape(runs, inner, lines, factor.shape[1]).astype(bf16)

    def gram_send(k):
        for d in range(1, inner):
            gram_a(k, d).start()

    def gram_sum(k):
        total = gp[k, :, place].astype(f32)
        for d in range(1, inner):
            gram_a(k, d).wait_recv()
            total = total + ga[k, d - 1].astype(f32)
        gacc[k] = total
        gmid[k] = total.astype(bf16)
        for i in range(runs):
            @pl.when(layer != k * runs + i)
            def _():
                gram_b(k, i).start()

    def span(q):
        return slice(q * size, (q + 1) * size)

    def entries(xs, xo, ys, yo, q, row_norms):
        ts, to = piv[col, span(q), :], piv[1 - col, span(q), :]
        cross = dot(xs, ts[:, :fw]) + dot(xo, to[:, :fw])
        schur = dot(ys, ts[:, fw:]) + dot(yo, to[:, fw:])
        return jnp.exp(-(row_norms + norms[q, 0:1, :] - 2.0 * cross) / feats) + schur / (3.0 * rank)

    def less(value, x, y, count):
        if count:
            return value - dot(x[:, :count * size], y[:, :count * size])
        return value

    def head(r):
        ps, po = piv[col, span(r), :], piv[1 - col, span(r), :]
        pnorm = norm(ps[:, :fw], po[:, :fw])
        norms[r] = jnp.transpose(jnp.broadcast_to(pnorm, (size, size)))

        def against(k):
            return entries(ps[:, :fw], po[:, :fw], ps[:, fw:], po[:, fw:], k, pnorm)

        for k in range(r):
            m = less(against(k), prow[r], prow[k], k)
            if k < r - 1:
                prow[r, :, span(k)] = exact(m, inv[k]).astype(bf16)
            else:
                ready[...] = m
        early[...] = less(against(r) + RIDGE_LEVEL * eye, prow[r], prow[r], max(r - 1, 0))

    def begin(r):
        if r:
            fresh = exact(ready[...], inv[r - 1]).astype(bf16)
            prow[r, :, span(r - 1)] = fresh
            inv[r] = early[...] - dot(fresh, fresh)
        else:
            inv[r] = early[...]

    def solve(r):
        out_ref[:, span(r)] = exact(columns[...], inv[r]).astype(bf16)

    def fill(r):
        ids = owners[r:r + 1, :] * here + slots[r:r + 1, :]
        value = entries(points[mine, :], other_points[...], factor[mine, :], other_factor[...], r, own_norm)
        value = value + jnp.where(own_ids == ids, RIDGE_LEVEL, 0.0)
        columns[...] = less(value, out_ref, prow[r], r)

    arrive(0)
    head(0)
    for q in range(panels):
        def early_hook():
            if q > 0:
                swap_panel(q - 1).start()

        def middle_hook():
            if q == 0 and panels > 3:
                layer_sum(3)
            if q > 0:
                gram_block(q - 1)
            if q == panels - 1:
                new_early()

        def late_hook():
            if q > 0:
                gram_send(q - 1)
            if q == panels - 1:
                for d in range(1, inner):
                    new_a(0, d).start()
            if q + 1 < panels:
                forward(q + 1)

        def last_hook():
            if q + 2 < panels:
                whole_sum(q + 2)
            if q > 1:
                gram_sum(q - 2)

        begin(q)
        if q:
            solve(q - 1)
        fill(q)
        factor_block(size, inv.at[q], rows, wide, {
            HOOKS[0] * BLOCK: early_hook, HOOKS[1] * BLOCK: middle_hook,
            HOOKS[2] * BLOCK: late_hook, HOOKS[3] * BLOCK: last_hook})
        if q + 1 < panels:
            arrive(q + 1)
            head(q + 1)
    solve(panels - 1)
    swap_panel(panels - 1).start()
    gram_block(panels - 1)
    gram_send(panels - 1)

    @pl.when(col == 1)
    def _():
        for source, which in ((out_ref, col), (other_ref, 1 - col)):
            own_cols[half_rows(which), width - size:] = source[:, count - size:]

    block = jnp.dot(level_t[count - size:, :], own_cols[...], preferred_element_type=f32) * scale_by
    nw[cut:] = block.reshape(outer - cut, inner, lines, width).astype(bf16)
    for d in range(1, inner):
        new_a(1, d).start()

    @pl.when(col == 1)
    def _():
        block = jnp.dot(level_t[:count - size, :], own_cols[:, width - size:], preferred_element_type=f32) * scale_by
        cw[...] = block.reshape(cut, inner, lines, size).astype(bf16)
        for d in range(1, inner):
            side_a(d).start()

    gram_sum(panels - 2)
    new_sum(0)
    gram_sum(panels - 1)
    new_sum(1)

    @pl.when(col == 1)
    def _():
        total = cw[:, place].astype(f32)
        for d in range(1, inner):
            side_a(d).wait_recv()
            total = total + ca[d - 1].astype(f32)
        cacc[...] = total
        cmid[...] = total.astype(bf16)
        for z in range(cut):
            @pl.when(layer != z)
            def _():
                side_b(z).start()

    total = gacc[layer // runs, layer % runs]
    for d in range(1, outer):
        gram_got(d).wait_recv()
        total = total + gb[d - 1].astype(f32)
    gram_old[...] = total
    total = nacc[layer]
    for d in range(1, outer):
        new_got(d).wait_recv()
        total = total + nb[d - 1].astype(f32)
    gram_new[...] = total

    @pl.when((col == 1) & (layer < cut))
    def _():
        total = gram_new[:, width - size:] + cacc[jnp.minimum(layer, cut - 1)]
        for d in range(1, outer):
            side_got(d).wait_recv()
            total = total + cb[d - 1].astype(f32)
        gram_new[:, width - size:] = total

    for d in range(1, inner):
        new_a(0, d).wait_send()
        new_a(1, d).wait_send()
    for z in range(outer):
        @pl.when(layer != z)
        def _():
            new_b(z).wait_send()

    @pl.when(col == 1)
    def _():
        for d in range(1, inner):
            side_a(d).wait_send()
        for z in range(cut):
            @pl.when(layer != z)
            def _():
                side_b(z).wait_send()

    for c in swap:
        c.wait_send()
    for q in range(panels):
        swap_panel(q).wait_send()
        for d in range(1, inner):
            within(q, d).wait_send()
            gram_a(q, d).wait_send()
        for i in range(runs):
            @pl.when(layer != q * runs + i)
            def _():
                gram_b(q, i).wait_send()
        for d in range(1, outer):
            along(q, d).wait_send()
        for d in range(1, inner):
            around(q, d).wait_send()
        for d in range(inner):
            across(q, d).wait_send()


def write_kernel(a, b, c, x, y, z, sems):
    copies = [pltpu.make_async_copy(s, d, sems.at[i]) for i, (s, d) in enumerate(((a, x), (b, y), (c, z)))]
    for c in copies:
        c.start()
    for c in copies:
        c.wait()


def body(points, factor, weights, pivot_slots, pivot_owners):
    here, fw = points.shape
    rank = factor.shape[1]
    panels, size = pivot_slots.shape
    rows = lax.axis_size("rows")
    count = panels * size
    chunk = count // rows
    width = fw + rank
    half = here // 2
    bf16, f32 = jnp.bfloat16, jnp.float32
    vm = pl.BlockSpec(memory_space=VMEM)
    hbm = pl.BlockSpec(memory_space=pl.ANY)
    sem = lambda *n: pltpu.SemaphoreType.DMA(n)
    limit = 60 * 1024 * 1024

    split = rows // panels if rows < panels * panels else panels
    layers = rows // split
    piece = size // split
    runs = layers // panels
    cut = layers - runs
    share = count // 2
    scale = size / math.sqrt(here * rows)
    outs = pl.pallas_call(
        functools.partial(panel_kernel, split, layers, scale),
        out_shape=(
            pltpu.VMEM((here, share), bf16), pltpu.VMEM((chunk, rank), f32), pltpu.VMEM((chunk, share), f32),
        ),
        in_specs=[vm, vm, hbm, hbm, vm], out_specs=(vm,) * 3, name="panels",
        scratch_shapes=[
            VMEM((half, count), bf16), VMEM((half, count), bf16), VMEM((count, here), bf16),
            VMEM((panels, runs, split, chunk, rank), bf16),
            VMEM((panels, split - 1, runs, chunk, rank), bf16),
            VMEM((panels, runs, chunk, rank), f32), VMEM((panels, runs, chunk, rank), bf16),
            VMEM((layers, chunk, rank), bf16),
            VMEM((layers, split, chunk, share), bf16),
            VMEM((split - 1, layers, chunk, share), bf16),
            VMEM((layers, chunk, share), f32), VMEM((layers, chunk, share), bf16),
            VMEM((layers - 1, chunk, share), bf16),
            VMEM((cut, split, chunk, size), bf16), VMEM((split - 1, cut, chunk, size), bf16),
            VMEM((cut, chunk, size), f32), VMEM((cut, chunk, size), bf16), VMEM((layers - 1, chunk, size), bf16),
            sem(panels, split - 1), sem(panels, split - 1), sem(panels, runs), sem(layers),
            sem(2, split - 1), sem(2, split - 1), sem(layers), sem(layers - 1),
            sem(split - 1), sem(split - 1), sem(cut), sem(layers - 1),
            VMEM((here, fw), bf16), VMEM((here, rank), bf16), sem(2),
            VMEM((count, width), bf16), VMEM((2, count, width), bf16),
            VMEM((half, fw), bf16), VMEM((half, rank), bf16),
            VMEM((panels, split - 1, piece, width), bf16),
            VMEM((panels, layers - 1, piece, width), bf16),
            VMEM((panels, piece, width), bf16),
            VMEM((panels, size, count), bf16),
            VMEM((panels, size, size), f32), VMEM((panels, size, size), f32),
            VMEM((size, size), f32), VMEM((size, size), f32), VMEM((half, size), f32),
            VMEM((4 * BLOCK, size), f32), VMEM((6 * BLOCK, BLOCK, size), f32),
            sem(panels, split - 1), sem(panels, split - 1), sem(panels, layers - 1), sem(panels, layers - 1),
            sem(panels), sem(panels), sem(panels, split - 1), sem(panels, split - 1),
            sem(panels, split), sem(panels, split), sem(2), sem(2),
        ],
        compiler_params=pltpu.CompilerParams(collective_id=0, has_side_effects=True, vmem_limit_bytes=limit),
    )(pivot_slots, pivot_owners, points, factor, weights.reshape(here // size, size))
    return pl.pallas_call(
        write_kernel,
        out_shape=(
            jax.ShapeDtypeStruct((here, share), bf16),
            jax.ShapeDtypeStruct((chunk, rank), f32),
            jax.ShapeDtypeStruct((chunk, share), f32),
        ),
        in_specs=[vm] * 3, out_specs=(hbm,) * 3, name="write",
        scratch_shapes=[sem(3)],
    )(*[pltpu.with_memory_space_constraint(v, pltpu.VMEM) for v in outs])


def solution(mesh):
    return jax.shard_map(
        body,
        mesh=mesh,
        in_specs=(P("rows", "cols"), P("rows", "cols"), P("rows"), P(), P()),
        out_specs=(P("rows", "cols"), P("rows", "cols"), P("rows", "cols")),
        check_vma=False,
    )
```

```python
import functools
import math

import jax
import jax.numpy as jnp
from jax import lax
from jax.experimental import pallas as pl
from jax.experimental.pallas import tpu as pltpu
from jax.sharding import PartitionSpec as P

RIDGE_LEVEL = 1.0
BLOCK = 8
HOOKS = (4, 8, 10, 12, 14)
VMEM = pltpu.VMEM
HIGH = lax.Precision.HIGHEST
NT = (((1,), (1,)), ((), ()))
TN = (((0,), (0,)), ((), ()))


def remote(src, dst, send, recv, row, col):
    return pltpu.make_async_remote_copy(
        src_ref=src, dst_ref=dst, send_sem=send, recv_sem=recv,
        device_id=(row, col), device_id_type=pl.DeviceIdType.MESH,
    )


def peers_of(me, col, inner, outer):
    place, layer = me % inner, me // inner
    peers = [(me, 1 - col)]
    peers += [(layer * inner + (place + d) % inner, col) for d in range(1, inner)]
    peers += [(((layer + d) % outer) * inner + place, col) for d in range(1, outer)]
    return peers


def pivot_chain(d):
    scales = []
    for k in range(0, BLOCK, 2):
        first = lax.rsqrt(d[k, k])
        both = lax.rsqrt(d[k, k] * d[k + 1, k + 1] - d[k + 1, k] * d[k + 1, k])
        scales += [first, both * (d[k, k] * first)]
        step = both * first
        for i in range(k + 2, BLOCK):
            d[i, k + 1] = (d[k, k] * d[i, k + 1] - d[i, k] * d[k + 1, k]) * step
        for i in range(k + 1, BLOCK):
            d[i, k] = d[i, k] * first
        for i in range(k + 2, BLOCK):
            for m in range(k + 2, i + 1):
                d[i, m] = d[i, m] - d[i, k] * d[m, k] - d[i, k + 1] * d[m, k + 1]
    return scales


def solve_rows(d, scales, z):
    for k in range(BLOCK):
        z[k] = z[k] * scales[k]
        for i in range(k + 1, BLOCK):
            z[i] = z[i] - d[i, k] * z[k]
    return z


def factor_block(size, x, rows, wide, hooks):
    deep = 2 * BLOCK
    lane = lax.broadcasted_iota(jnp.int32, (BLOCK, size), 1)
    line = lax.broadcasted_iota(jnp.int32, (BLOCK, size), 0)

    def full(ref, i):
        return jnp.broadcast_to(ref[i:i + 1, :], (BLOCK, size))

    for first in range(0, size, deep):
        if first in hooks:
            hooks[first]()
        turn = first // deep % 2
        base, at = 3 * BLOCK * turn, deep * turn
        middle, after = first + BLOCK, first + deep
        inside = (lane >= first) & (lane < after)
        top = x[first:middle, :]
        low = x[middle:after, :]
        for k in range(BLOCK):
            for slot, part, spot in ((0, top, first + k), (1, low, first + k), (2, low, middle + k)):
                wide[base + slot * BLOCK + k] = jnp.broadcast_to(part[:, spot:spot + 1], (BLOCK, size))
        d = {(i, k): full(wide.at[base + k], i) for i in range(BLOCK) for k in range(i + 1)}
        scales = pivot_chain(d)
        left = []
        for k in range(BLOCK):
            w = wide[base + BLOCK + k]
            for m in range(k):
                w = w - d[k, m] * left[m]
            left.append(w * scales[k])
            wide[base + BLOCK + k] = left[k]
        z = [jnp.where(inside, jnp.where(lane == first + i, 1.0, 0.0), full(x, first + i)) for i in range(BLOCK)]
        z = solve_rows(d, scales, z)
        under = jnp.where(inside, jnp.where(lane == middle + line, 1.0, 0.0), low)
        for k in range(BLOCK):
            under = under - left[k] * z[k]
            rows[at + k:at + k + 1, :] = z[k][0:1, :]
        x[middle:after, :] = under
        for m in range(BLOCK):
            v = wide[base + 2 * BLOCK + m]
            for k in range(BLOCK):
                v = v - left[k] * full(wide.at[base + BLOCK + k], m)
            wide[base + 2 * BLOCK + m] = v
        d = {(i, k): full(wide.at[base + 2 * BLOCK + k], i) for i in range(BLOCK) for k in range(i + 1)}
        scales = pivot_chain(d)
        z = solve_rows(d, scales, [full(x, middle + i) for i in range(BLOCK)])
        for k in range(BLOCK):
            rows[at + BLOCK + k:at + BLOCK + k + 1, :] = z[k][0:1, :]
        done = rows[at:at + deep, :]
        x[first:after, :] = jnp.where(lax.broadcasted_iota(jnp.int32, (deep, size), 1) < after, done, 0.0)
        if after < size:
            upper = jnp.transpose(done)
            for start, stop in ((after, after + deep), (after + deep, size)):
                if start < stop:
                    spots = lax.broadcasted_iota(jnp.int32, (stop - start, size), 1)
                    rest = jnp.where((spots >= first) & (spots < after), 0.0, x[start:stop, :])
                    for k in range(deep):
                        rest = rest - upper[start:stop, k:k + 1] * rows[at + k:at + k + 1, :]
                    x[start:stop, :] = rest


def panel_kernel(inner, outer, scale_by, slots, owners, points_in, factor_in, weights, own_cols, gram_old, gram_new,
                 out_ref, other_ref, level_t, gp, ga, gacc, gmid, gb, nw, na, nacc, nmid, nb,
                 cw, ca, cacc, cmid, cb,
                 ga_send, ga_recv, gb_send, gb_recv, na_send, na_recv, nb_send, nb_recv,
                 ca_send, ca_recv, cb_send, cb_recv,
                 points, factor, load, part, piv, other_points, other_factor, buf_a, buf_b, acc, mid,
                 prow, inv, norms, early, ready, columns, rows, wide,
                 a_send, a_recv, b_send, b_recv, f_send, f_recv,
                 d_send, d_recv, e_send, e_recv, x_send, x_recv):
    me = lax.axis_index("rows")
    col = lax.axis_index("cols")
    place, layer = me % inner, me // inner
    panels, size = slots.shape
    here, fw = points.shape
    half = here // 2
    feats, rank = 2 * fw, 2 * factor.shape[1]
    chunk = size // inner
    f32, bf16 = jnp.float32, jnp.bfloat16

    loads = [
        pltpu.make_async_copy(points_in, points, load.at[0]),
        pltpu.make_async_copy(factor_in, factor, load.at[1]),
    ]
    for c in loads:
        c.start()
    barrier = pltpu.get_barrier_semaphore()
    peers = peers_of(me, col, inner, outer)
    for peer in peers:
        pl.semaphore_signal(barrier, inc=1, device_id=peer, device_id_type=pl.DeviceIdType.MESH)

    def piece(q, p):
        return pl.ds(pl.multiple_of(q * size + p * chunk, chunk), chunk)

    def turned(row):
        return jnp.transpose(jnp.broadcast_to(row, (size, size)))

    spots = lax.broadcasted_iota(jnp.int32, (size, here), 1) + me * here

    def gather(q):
        ids = (owners[q:q + 1, :] * here + slots[q:q + 1, :]).astype(f32)
        hot = jnp.where(spots == turned(ids)[:, 0:1].astype(jnp.int32), 1.0, 0.0).astype(bf16)
        span = slice(q * size, (q + 1) * size)
        part[span, :fw] = jnp.dot(hot, points[...], preferred_element_type=f32).astype(bf16)
        part[span, fw:] = jnp.dot(hot, factor[...], preferred_element_type=f32).astype(bf16)

    def within(q, d):
        p = (place + d) % inner
        return remote(part.at[piece(q, p)], buf_a.at[q, d - 1], a_send.at[q, d - 1], a_recv.at[q, d - 1],
                      layer * inner + p, col)

    def along(q, d):
        return remote(acc.at[q], buf_b.at[q, d - 1], b_send.at[q, d - 1], b_recv.at[q, d - 1],
                      ((layer + d) % outer) * inner + place, col)

    def around(q, d):
        it = piv.at[col, piece(q, place)]
        return remote(it, it, d_send.at[q, d - 1], d_recv.at[q, d - 1], layer * inner + (place + d) % inner, col)

    def across(q, d):
        it = piv.at[col, piece(q, (place + inner - d) % inner)]
        return remote(it, it, e_send.at[q, d], e_recv.at[q, d], me, 1 - col)

    def swap_panel(q):
        span = slice(q * size, (q + 1) * size)
        return remote(out_ref.at[:, span], other_ref.at[:, span], f_send.at[q], f_recv.at[q], me, 1 - col)

    def layer_start(q):
        for d in range(1, inner):
            within(q, d).start()

    steps = (outer - 1).bit_length()
    paired = outer == 1 << steps

    def twice(q, j):
        away = layer + (1 << j) - (2 << j) * (layer // (1 << j) % 2)
        source = mid.at[q, j - 1] if j else acc.at[q]
        return remote(source, buf_b.at[q, j], b_send.at[q, j], b_recv.at[q, j], away * inner + place, col)

    def sends_b(q):
        if q and paired:
            return [twice(q, j) for j in range(steps)]
        return [along(q, d) for d in range(1, outer)]

    def layer_sum(q):
        total = part[piece(q, place), :]
        for d in range(1, inner):
            within(q, d).wait_recv()
            total = total + buf_a[q, d - 1]
        acc[q] = total
        for c in sends_b(q)[:1 if q and paired else outer]:
            c.start()

    def between(q):
        if paired:
            total = acc[q]
            for j in range(1, steps):
                twice(q, j - 1).wait_recv()
                total = total + buf_b[q, j - 1]
                mid[q, j - 1] = total
                twice(q, j).start()

    def whole_sum(q):
        if q and paired:
            twice(q, steps - 1).wait_recv()
            total = (mid[q, steps - 2] if steps > 1 else acc[q]) + buf_b[q, steps - 1]
        else:
            total = acc[q]
            for d in range(1, outer):
                along(q, d).wait_recv()
                total = total + buf_b[q, d - 1]
        piv[col, piece(q, place)] = total
        for d in range(1, inner):
            around(q, d).start()
        across(q, 0).start()

    def forward(q):
        for d in range(1, inner):
            around(q, d).wait_recv()
            across(q, d).start()

    def arrive(q):
        for d in range(inner):
            across(q, d).wait_recv()

    theirs = pl.ds(pl.multiple_of((1 - col) * half, 16), half)
    swap = [
        remote(points.at[theirs], other_points, x_send.at[0], x_recv.at[0], me, 1 - col),
        remote(factor.at[theirs], other_factor, x_send.at[1], x_recv.at[1], me, 1 - col),
    ]

    for c in loads:
        c.wait()
    gather(0)
    pl.semaphore_wait(barrier, len(peers))
    layer_start(0)
    for c in swap:
        c.start()
    for q in range(1, panels):
        gather(q)
        layer_start(q)
    for q in range(panels):
        layer_sum(q)
        if q == 2:
            between(1)

    def norm(x, y):
        x, y = x.astype(f32), y.astype(f32)
        return jnp.sum(x * x, axis=1, keepdims=True) + jnp.sum(y * y, axis=1, keepdims=True)

    def dot(x, y):
        return lax.dot_general(x, y, NT, preferred_element_type=f32)

    def exact(x, y):
        return lax.dot_general(x, y, NT, precision=HIGH, preferred_element_type=f32)

    for c in swap:
        c.wait_recv()
    mine = pl.ds(pl.multiple_of(col * half, 16), half)
    own_norm = norm(points[mine, :], other_points[...])
    own_ids = lax.broadcasted_iota(jnp.int32, (half, size), 0) + (me * here + col * half)
    same = lax.broadcasted_iota(jnp.int32, (size, size), 0) == lax.broadcasted_iota(jnp.int32, (size, size), 1)
    eye = jnp.where(same, 1.0, 0.0)

    whole_sum(0)
    for q in range(2, panels):
        between(q)
    forward(0)
    whole_sum(1)

    runs = gp.shape[1]
    lines = gp.shape[3]
    width = own_cols.shape[1]

    def gram_a(k, d):
        p = (place + d) % inner
        return remote(gp.at[k, :, p], ga.at[k, d - 1], ga_send.at[k, d - 1], ga_recv.at[k, d - 1],
                      layer * inner + p, col)

    def gram_b(k, i):
        target = k * runs + i
        slot = (layer - target + 2 * outer - 1) % outer
        return remote(gmid.at[k, i], gb.at[slot], gb_send.at[k, i], gb_recv.at[slot], target * inner + place, col)

    def gram_got(d):
        return remote(gmid.at[0, 0], gb.at[d - 1], gb_send.at[0, 0], gb_recv.at[d - 1],
                      ((layer + d) % outer) * inner + place, col)

    cut = outer - runs
    count = panels * size

    def half_rows(which):
        return pl.ds(pl.multiple_of(which * half, 16), half)

    def slot_of(z):
        return (layer - z + 2 * outer - 1) % outer

    def new_a(late, d):
        p = (place + d) % inner
        rows_of = slice(cut, outer) if late else slice(0, cut)
        return remote(nw.at[rows_of, p], na.at[d - 1, rows_of], na_send.at[late, d - 1], na_recv.at[late, d - 1],
                      layer * inner + p, col)

    def new_b(z):
        return remote(nmid.at[z], nb.at[slot_of(z)], nb_send.at[z], nb_recv.at[slot_of(z)], z * inner + place, col)

    def new_got(d):
        return remote(nmid.at[0], nb.at[d - 1], nb_send.at[0], nb_recv.at[d - 1],
                      ((layer + d) % outer) * inner + place, col)

    def side_a(d):
        p = (place + d) % inner
        return remote(cw.at[:, p], ca.at[d - 1], ca_send.at[d - 1], ca_recv.at[d - 1], layer * inner + p, col)

    def side_b(z):
        return remote(cmid.at[z], cb.at[slot_of(z)], cb_send.at[z], cb_recv.at[slot_of(z)], z * inner + place, col)

    def side_got(d):
        return remote(cmid.at[0], cb.at[d - 1], cb_send.at[0], cb_recv.at[d - 1],
                      ((layer + d) % outer) * inner + place, col)

    def new_early():
        for source, which in ((out_ref, col), (other_ref, 1 - col)):
            own_cols[half_rows(which), :width - size] = source[:, pl.ds(pl.multiple_of(col * width, 128), width - size)]

        @pl.when(col == 0)
        def _():
            for source, which in ((out_ref, col), (other_ref, 1 - col)):
                own_cols[half_rows(which), width - size:] = source[:, width - size:width]

        @pl.when(col == 1)
        def _():
            own_cols[:, width - size:] = jnp.zeros((here, size), bf16)

        block = jnp.dot(level_t[:count - size, :], own_cols[...], preferred_element_type=f32) * scale_by
        nw[:cut] = block.reshape(cut, inner, lines, width).astype(bf16)

    def new_sum(late):
        rows_of = slice(cut, outer) if late else slice(0, cut)
        total = nw[rows_of, place].astype(f32)
        for d in range(1, inner):
            new_a(late, d).wait_recv()
            total = total + na[d - 1, rows_of].astype(f32)
        nacc[rows_of] = total
        nmid[rows_of] = total.astype(bf16)
        for z in range(outer)[rows_of]:
            @pl.when(layer != z)
            def _():
                new_b(z).start()

    def gram_block(k):
        lanes = slice(k * size, (k + 1) * size)

        def part_of(source, which):
            for i in range(half // size):
                level = turned(weights[pl.ds(which * (half // size) + i, 1), :])[:, 0:1]
                block = source[i * size:(i + 1) * size, lanes].astype(f32) * level
                first = pl.multiple_of(which * half + i * size, size)
                level_t[lanes, pl.ds(first, size)] = jnp.transpose(block).astype(bf16)
            spots = pl.ds(pl.multiple_of(which * half, size), half)
            return jnp.dot(level_t[lanes, spots], factor[half_rows(which), :], preferred_element_type=f32)

        block = part_of(out_ref, col)
        swap_panel(k).wait_recv()
        block = (block + part_of(other_ref, 1 - col)) * scale_by
        gp[k] = block.reshape(runs, inner, lines, factor.shape[1]).astype(bf16)

    def gram_send(k):
        for d in range(1, inner):
            gram_a(k, d).start()

    def gram_sum(k):
        total = gp[k, :, place].astype(f32)
        for d in range(1, inner):
            gram_a(k, d).wait_recv()
            total = total + ga[k, d - 1].astype(f32)
        gacc[k] = total
        gmid[k] = total.astype(bf16)
        for i in range(runs):
            @pl.when(layer != k * runs + i)
            def _():
                gram_b(k, i).start()

    def span(q):
        return slice(q * size, (q + 1) * size)

    def entries(xs, xo, ys, yo, q, row_norms):
        ts, to = piv[col, span(q), :], piv[1 - col, span(q), :]
        cross = dot(xs, ts[:, :fw]) + dot(xo, to[:, :fw])
        schur = dot(ys, ts[:, fw:]) + dot(yo, to[:, fw:])
        return jnp.exp(-(row_norms + norms[q, 0:1, :] - 2.0 * cross) / feats) + schur / (3.0 * rank)

    def less(value, x, y, count):
        if count:
            return value - dot(x[:, :count * size], y[:, :count * size])
        return value

    def head(r):
        ps, po = piv[col, span(r), :], piv[1 - col, span(r), :]
        pnorm = norm(ps[:, :fw], po[:, :fw])
        norms[r] = jnp.transpose(jnp.broadcast_to(pnorm, (size, size)))

        def against(k):
            return entries(ps[:, :fw], po[:, :fw], ps[:, fw:], po[:, fw:], k, pnorm)

        for k in range(r):
            m = less(against(k), prow[r], prow[k], k)
            if k < r - 1:
                prow[r, :, span(k)] = exact(m, inv[k]).astype(bf16)
            else:
                ready[...] = m
        early[...] = less(against(r) + RIDGE_LEVEL * eye, prow[r], prow[r], max(r - 1, 0))

    def begin(r):
        if r:
            fresh = exact(ready[...], inv[r - 1]).astype(bf16)
            prow[r, :, span(r - 1)] = fresh
            inv[r] = early[...] - dot(fresh, fresh)
        else:
            inv[r] = early[...]

    def solve(r):
        out_ref[:, span(r)] = exact(columns[...], inv[r]).astype(bf16)

    def fill(r):
        ids = owners[r:r + 1, :] * here + slots[r:r + 1, :]
        value = entries(points[mine, :], other_points[...], factor[mine, :], other_factor[...], r, own_norm)
        value = value + jnp.where(own_ids == ids, RIDGE_LEVEL, 0.0)
        columns[...] = less(value, out_ref, prow[r], r)

    arrive(0)
    head(0)
    for q in range(panels):
        def hook_a():
            if q > 0:
                swap_panel(q - 1).start()
            if q == 0:
                whole_sum(2)
            if q == 1:
                forward(2)

        def hook_b():
            if q > 0:
                gram_block(q - 1)
            if q == panels - 1:
                new_early()

        def hook_c():
            if q == 0:
                forward(1)
                whole_sum(3)
            elif q + 1 < panels:
                arrive(q + 1)
                head(q + 1)

        def hook_d():
            if q > 0:
                gram_send(q - 1)
            if q == panels - 1:
                for d in range(1, inner):
                    new_a(0, d).start()
            if q == 1:
                forward(3)

        def hook_e():
            if q == 0:
                arrive(1)
                head(1)
            if q > 1:
                gram_sum(q - 2)

        begin(q)
        if q:
            solve(q - 1)
        fill(q)
        hooks = dict(zip((at * BLOCK for at in HOOKS), (hook_a, hook_b, hook_c, hook_d, hook_e)))
        factor_block(size, inv.at[q], rows, wide, hooks)
    solve(panels - 1)
    swap_panel(panels - 1).start()
    gram_block(panels - 1)
    gram_send(panels - 1)

    @pl.when(col == 1)
    def _():
        for source, which in ((out_ref, col), (other_ref, 1 - col)):
            own_cols[half_rows(which), width - size:] = source[:, count - size:]

    block = jnp.dot(level_t[count - size:, :], own_cols[...], preferred_element_type=f32) * scale_by
    nw[cut:] = block.reshape(outer - cut, inner, lines, width).astype(bf16)
    for d in range(1, inner):
        new_a(1, d).start()

    @pl.when(col == 1)
    def _():
        block = jnp.dot(level_t[:count - size, :], own_cols[:, width - size:], preferred_element_type=f32) * scale_by
        cw[...] = block.reshape(cut, inner, lines, size).astype(bf16)
        for d in range(1, inner):
            side_a(d).start()

    gram_sum(panels - 2)
    new_sum(0)
    gram_sum(panels - 1)
    new_sum(1)

    @pl.when(col == 1)
    def _():
        total = cw[:, place].astype(f32)
        for d in range(1, inner):
            side_a(d).wait_recv()
            total = total + ca[d - 1].astype(f32)
        cacc[...] = total
        cmid[...] = total.astype(bf16)
        for z in range(cut):
            @pl.when(layer != z)
            def _():
                side_b(z).start()

    total = gacc[layer // runs, layer % runs]
    for d in range(1, outer):
        gram_got(d).wait_recv()
        total = total + gb[d - 1].astype(f32)
    gram_old[...] = total
    total = nacc[layer]
    for d in range(1, outer):
        new_got(d).wait_recv()
        total = total + nb[d - 1].astype(f32)
    gram_new[...] = total

    @pl.when((col == 1) & (layer < cut))
    def _():
        total = gram_new[:, width - size:] + cacc[jnp.minimum(layer, cut - 1)]
        for d in range(1, outer):
            side_got(d).wait_recv()
            total = total + cb[d - 1].astype(f32)
        gram_new[:, width - size:] = total

    for d in range(1, inner):
        new_a(0, d).wait_send()
        new_a(1, d).wait_send()
    for z in range(outer):
        @pl.when(layer != z)
        def _():
            new_b(z).wait_send()

    @pl.when(col == 1)
    def _():
        for d in range(1, inner):
            side_a(d).wait_send()
        for z in range(cut):
            @pl.when(layer != z)
            def _():
                side_b(z).wait_send()

    for c in swap:
        c.wait_send()
    for q in range(panels):
        swap_panel(q).wait_send()
        for d in range(1, inner):
            within(q, d).wait_send()
            gram_a(q, d).wait_send()
        for i in range(runs):
            @pl.when(layer != q * runs + i)
            def _():
                gram_b(q, i).wait_send()
        for c in sends_b(q):
            c.wait_send()
        for d in range(1, inner):
            around(q, d).wait_send()
        for d in range(inner):
            across(q, d).wait_send()


def write_kernel(a, b, c, x, y, z, sems):
    copies = [pltpu.make_async_copy(s, d, sems.at[i]) for i, (s, d) in enumerate(((a, x), (b, y), (c, z)))]
    for c in copies:
        c.start()
    for c in copies:
        c.wait()


def body(points, factor, weights, pivot_slots, pivot_owners):
    here, fw = points.shape
    rank = factor.shape[1]
    panels, size = pivot_slots.shape
    rows = lax.axis_size("rows")
    count = panels * size
    chunk = count // rows
    width = fw + rank
    half = here // 2
    bf16, f32 = jnp.bfloat16, jnp.float32
    vm = pl.BlockSpec(memory_space=VMEM)
    hbm = pl.BlockSpec(memory_space=pl.ANY)
    sem = lambda *n: pltpu.SemaphoreType.DMA(n)
    limit = 60 * 1024 * 1024

    split = rows // panels if rows < panels * panels else panels
    layers = rows // split
    piece = size // split
    runs = layers // panels
    cut = layers - runs
    share = count // 2
    scale = size / math.sqrt(here * rows)
    outs = pl.pallas_call(
        functools.partial(panel_kernel, split, layers, scale),
        out_shape=(
            pltpu.VMEM((here, share), bf16), pltpu.VMEM((chunk, rank), f32), pltpu.VMEM((chunk, share), f32),
        ),
        in_specs=[vm, vm, hbm, hbm, vm], out_specs=(vm,) * 3, name="panels",
        scratch_shapes=[
            VMEM((half, count), bf16), VMEM((half, count), bf16), VMEM((count, here), bf16),
            VMEM((panels, runs, split, chunk, rank), bf16),
            VMEM((panels, split - 1, runs, chunk, rank), bf16),
            VMEM((panels, runs, chunk, rank), f32), VMEM((panels, runs, chunk, rank), bf16),
            VMEM((layers, chunk, rank), bf16),
            VMEM((layers, split, chunk, share), bf16),
            VMEM((split - 1, layers, chunk, share), bf16),
            VMEM((layers, chunk, share), f32), VMEM((layers, chunk, share), bf16),
            VMEM((layers - 1, chunk, share), bf16),
            VMEM((cut, split, chunk, size), bf16), VMEM((split - 1, cut, chunk, size), bf16),
            VMEM((cut, chunk, size), f32), VMEM((cut, chunk, size), bf16), VMEM((layers - 1, chunk, size), bf16),
            sem(panels, split - 1), sem(panels, split - 1), sem(panels, runs), sem(layers),
            sem(2, split - 1), sem(2, split - 1), sem(layers), sem(layers - 1),
            sem(split - 1), sem(split - 1), sem(cut), sem(layers - 1),
            VMEM((here, fw), bf16), VMEM((here, rank), bf16), sem(2),
            VMEM((count, width), bf16), VMEM((2, count, width), bf16),
            VMEM((half, fw), bf16), VMEM((half, rank), bf16),
            VMEM((panels, split - 1, piece, width), bf16),
            VMEM((panels, layers - 1, piece, width), bf16),
            VMEM((panels, piece, width), bf16), VMEM((panels, (layers - 1).bit_length(), piece, width), bf16),
            VMEM((panels, size, count), bf16),
            VMEM((panels, size, size), f32), VMEM((panels, size, size), f32),
            VMEM((size, size), f32), VMEM((size, size), f32), VMEM((half, size), f32),
            VMEM((4 * BLOCK, size), f32), VMEM((6 * BLOCK, BLOCK, size), f32),
            sem(panels, split - 1), sem(panels, split - 1), sem(panels, layers - 1), sem(panels, layers - 1),
            sem(panels), sem(panels), sem(panels, split - 1), sem(panels, split - 1),
            sem(panels, split), sem(panels, split), sem(2), sem(2),
        ],
        compiler_params=pltpu.CompilerParams(collective_id=0, has_side_effects=True, vmem_limit_bytes=limit),
    )(pivot_slots, pivot_owners, points, factor, weights.reshape(here // size, size))
    return pl.pallas_call(
        write_kernel,
        out_shape=(
            jax.ShapeDtypeStruct((here, share), bf16),
            jax.ShapeDtypeStruct((chunk, rank), f32),
            jax.ShapeDtypeStruct((chunk, share), f32),
        ),
        in_specs=[vm] * 3, out_specs=(hbm,) * 3, name="write",
        scratch_shapes=[sem(3)],
    )(*[pltpu.with_memory_space_constraint(v, pltpu.VMEM) for v in outs])


def solution(mesh):
    return jax.shard_map(
        body,
        mesh=mesh,
        in_specs=(P("rows", "cols"), P("rows", "cols"), P("rows"), P(), P()),
        out_specs=(P("rows", "cols"), P("rows", "cols"), P("rows", "cols")),
        check_vma=False,
    )
```

```python
import functools
import math

import jax
import jax.numpy as jnp
from jax import lax
from jax.experimental import pallas as pl
from jax.experimental.pallas import tpu as pltpu
from jax.sharding import PartitionSpec as P

RIDGE_LEVEL = 1.0
BLOCK = 8
HOOKS = (4, 8, 10, 12, 14)
PLACES = (0, 1, 1, 3, 4)
VMEM = pltpu.VMEM
HIGH = lax.Precision.HIGHEST
NT = (((1,), (1,)), ((), ()))
TN = (((0,), (0,)), ((), ()))


def remote(src, dst, send, recv, row, col):
    return pltpu.make_async_remote_copy(
        src_ref=src, dst_ref=dst, send_sem=send, recv_sem=recv,
        device_id=(row, col), device_id_type=pl.DeviceIdType.MESH,
    )


def peers_of(me, col, inner, outer):
    place, layer = me % inner, me // inner
    peers = [(me, 1 - col)]
    peers += [(layer * inner + (place + d) % inner, col) for d in range(1, inner)]
    peers += [(((layer + d) % outer) * inner + place, col) for d in range(1, outer)]
    return peers


def pivot_chain(d):
    scales = []
    for k in range(0, BLOCK, 2):
        first = lax.rsqrt(d[k, k])
        both = lax.rsqrt(d[k, k] * d[k + 1, k + 1] - d[k + 1, k] * d[k + 1, k])
        scales += [first, both * (d[k, k] * first)]
        step = both * first
        for i in range(k + 2, BLOCK):
            d[i, k + 1] = (d[k, k] * d[i, k + 1] - d[i, k] * d[k + 1, k]) * step
        for i in range(k + 1, BLOCK):
            d[i, k] = d[i, k] * first
        for i in range(k + 2, BLOCK):
            for m in range(k + 2, i + 1):
                d[i, m] = d[i, m] - d[i, k] * d[m, k] - d[i, k + 1] * d[m, k + 1]
    return scales


def solve_rows(d, scales, z):
    for k in range(BLOCK):
        z[k] = z[k] * scales[k]
        for i in range(k + 1, BLOCK):
            z[i] = z[i] - d[i, k] * z[k]
    return z


def factor_block(size, x, rows, wide, hooks):
    deep = 2 * BLOCK
    lane = lax.broadcasted_iota(jnp.int32, (BLOCK, size), 1)
    line = lax.broadcasted_iota(jnp.int32, (BLOCK, size), 0)

    def full(ref, i):
        return jnp.broadcast_to(ref[i:i + 1, :], (BLOCK, size))

    for first in range(0, size, deep):
        if first in hooks:
            hooks[first]()
        turn = first // deep % 2
        base, at = 3 * BLOCK * turn, deep * turn
        middle, after = first + BLOCK, first + deep
        inside = (lane >= first) & (lane < after)
        top = x[first:middle, :]
        low = x[middle:after, :]
        for k in range(BLOCK):
            for slot, part, spot in ((0, top, first + k), (1, low, first + k), (2, low, middle + k)):
                wide[base + slot * BLOCK + k] = jnp.broadcast_to(part[:, spot:spot + 1], (BLOCK, size))
        d = {(i, k): full(wide.at[base + k], i) for i in range(BLOCK) for k in range(i + 1)}
        scales = pivot_chain(d)
        left = []
        for k in range(BLOCK):
            w = wide[base + BLOCK + k]
            for m in range(k):
                w = w - d[k, m] * left[m]
            left.append(w * scales[k])
            wide[base + BLOCK + k] = left[k]
        z = [jnp.where(inside, jnp.where(lane == first + i, 1.0, 0.0), full(x, first + i)) for i in range(BLOCK)]
        z = solve_rows(d, scales, z)
        under = jnp.where(inside, jnp.where(lane == middle + line, 1.0, 0.0), low)
        for k in range(BLOCK):
            under = under - left[k] * z[k]
            rows[at + k:at + k + 1, :] = z[k][0:1, :]
        x[middle:after, :] = under
        for m in range(BLOCK):
            v = wide[base + 2 * BLOCK + m]
            for k in range(BLOCK):
                v = v - left[k] * full(wide.at[base + BLOCK + k], m)
            wide[base + 2 * BLOCK + m] = v
        d = {(i, k): full(wide.at[base + 2 * BLOCK + k], i) for i in range(BLOCK) for k in range(i + 1)}
        scales = pivot_chain(d)
        z = solve_rows(d, scales, [full(x, middle + i) for i in range(BLOCK)])
        for k in range(BLOCK):
            rows[at + BLOCK + k:at + BLOCK + k + 1, :] = z[k][0:1, :]
        done = rows[at:at + deep, :]
        x[first:after, :] = jnp.where(lax.broadcasted_iota(jnp.int32, (deep, size), 1) < after, done, 0.0)
        if after < size:
            upper = jnp.transpose(done)
            for start, stop in ((after, after + deep), (after + deep, size)):
                if start < stop:
                    spots = lax.broadcasted_iota(jnp.int32, (stop - start, size), 1)
                    rest = jnp.where((spots >= first) & (spots < after), 0.0, x[start:stop, :])
                    for k in range(deep):
                        rest = rest - upper[start:stop, k:k + 1] * rows[at + k:at + k + 1, :]
                    x[start:stop, :] = rest


def panel_kernel(inner, outer, scale_by, slots, owners, points_in, factor_in, weights, own_cols, gram_old, gram_new,
                 out_ref, other_ref, level_t, gp, ga, gacc, gmid, gb, nw, na, nacc, nmid, nb,
                 cw, ca, cacc, cmid, cb,
                 ga_send, ga_recv, gb_send, gb_recv, na_send, na_recv, nb_send, nb_recv,
                 ca_send, ca_recv, cb_send, cb_recv,
                 points, factor, load, part, piv, other_points, other_factor, buf_a, buf_b, acc, mid,
                 prow, inv, norms, early, ready, columns, levels, rows, wide,
                 a_send, a_recv, b_send, b_recv, f_send, f_recv,
                 d_send, d_recv, e_send, e_recv, x_send, x_recv):
    me = lax.axis_index("rows")
    col = lax.axis_index("cols")
    place, layer = me % inner, me // inner
    panels, size = slots.shape
    here, fw = points.shape
    half = here // 2
    feats, rank = 2 * fw, 2 * factor.shape[1]
    chunk = size // inner
    f32, bf16 = jnp.float32, jnp.bfloat16

    loads = [
        pltpu.make_async_copy(points_in, points, load.at[0]),
        pltpu.make_async_copy(factor_in, factor, load.at[1]),
    ]
    for c in loads:
        c.start()
    barrier = pltpu.get_barrier_semaphore()
    peers = peers_of(me, col, inner, outer)
    for peer in peers:
        pl.semaphore_signal(barrier, inc=1, device_id=peer, device_id_type=pl.DeviceIdType.MESH)

    def piece(q, p):
        return pl.ds(pl.multiple_of(q * size + p * chunk, chunk), chunk)

    def turned(row):
        return jnp.transpose(jnp.broadcast_to(row, (size, size)))

    spots = lax.broadcasted_iota(jnp.int32, (size, here), 1) + me * here

    def gather(q):
        ids = (owners[q:q + 1, :] * here + slots[q:q + 1, :]).astype(f32)
        hot = jnp.where(spots == turned(ids)[:, 0:1].astype(jnp.int32), 1.0, 0.0).astype(bf16)
        span = slice(q * size, (q + 1) * size)
        part[span, :fw] = jnp.dot(hot, points[...], preferred_element_type=f32).astype(bf16)
        part[span, fw:] = jnp.dot(hot, factor[...], preferred_element_type=f32).astype(bf16)

    def within(q, d):
        p = (place + d) % inner
        return remote(part.at[piece(q, p)], buf_a.at[q, d - 1], a_send.at[q, d - 1], a_recv.at[q, d - 1],
                      layer * inner + p, col)

    def along(q, d):
        return remote(acc.at[q], buf_b.at[q, d - 1], b_send.at[q, d - 1], b_recv.at[q, d - 1],
                      ((layer + d) % outer) * inner + place, col)

    def around(q, d):
        it = piv.at[col, piece(q, place)]
        return remote(it, it, d_send.at[q, d - 1], d_recv.at[q, d - 1], layer * inner + (place + d) % inner, col)

    def across(q, d):
        it = piv.at[col, piece(q, (place + inner - d) % inner)]
        return remote(it, it, e_send.at[q, d], e_recv.at[q, d], me, 1 - col)

    def swap_panel(q):
        span = slice(q * size, (q + 1) * size)
        return remote(out_ref.at[:, span], other_ref.at[:, span], f_send.at[q], f_recv.at[q], me, 1 - col)

    def layer_start(q):
        for d in range(1, inner):
            within(q, d).start()

    steps = (outer - 1).bit_length()
    paired = outer == 1 << steps

    def twice(q, j):
        away = layer + (1 << j) - (2 << j) * (layer // (1 << j) % 2)
        source = mid.at[q, j - 1] if j else acc.at[q]
        return remote(source, buf_b.at[q, j], b_send.at[q, j], b_recv.at[q, j], away * inner + place, col)

    def sends_b(q, count=None):
        if q and paired:
            return [twice(q, j) for j in range(count or steps)]
        return [along(q, d) for d in range(1, outer)]

    def layer_sum(q):
        total = part[piece(q, place), :]
        for d in range(1, inner):
            within(q, d).wait_recv()
            total = total + buf_a[q, d - 1]
        acc[q] = total
        for c in sends_b(q, 1):
            c.start()

    def between(q):
        if paired:
            total = acc[q]
            for j in range(1, steps):
                twice(q, j - 1).wait_recv()
                total = total + buf_b[q, j - 1]
                mid[q, j - 1] = total
                twice(q, j).start()

    def whole_sum(q):
        if q and paired:
            twice(q, steps - 1).wait_recv()
            total = (mid[q, steps - 2] if steps > 1 else acc[q]) + buf_b[q, steps - 1]
        else:
            total = acc[q]
            for d in range(1, outer):
                along(q, d).wait_recv()
                total = total + buf_b[q, d - 1]
        piv[col, piece(q, place)] = total
        for d in range(1, inner):
            around(q, d).start()
        across(q, 0).start()

    def forward(q):
        for d in range(1, inner):
            around(q, d).wait_recv()
            across(q, d).start()

    def arrive(q):
        for d in range(inner):
            across(q, d).wait_recv()

    theirs = pl.ds(pl.multiple_of((1 - col) * half, 16), half)
    swap = [
        remote(points.at[theirs], other_points, x_send.at[0], x_recv.at[0], me, 1 - col),
        remote(factor.at[theirs], other_factor, x_send.at[1], x_recv.at[1], me, 1 - col),
    ]

    for c in loads:
        c.wait()
    gather(0)
    pl.semaphore_wait(barrier, len(peers))
    layer_start(0)
    for c in swap:
        c.start()
    for q in range(1, panels):
        gather(q)
        layer_start(q)
    for q in range(panels):
        layer_sum(q)
        if q == 2:
            between(1)

    def norm(x, y):
        x, y = x.astype(f32), y.astype(f32)
        return jnp.sum(x * x, axis=1, keepdims=True) + jnp.sum(y * y, axis=1, keepdims=True)

    def dot(x, y):
        return lax.dot_general(x, y, NT, preferred_element_type=f32)

    def exact(x, y):
        return lax.dot_general(x, y, NT, precision=HIGH, preferred_element_type=f32)

    for c in swap:
        c.wait_recv()
    mine = pl.ds(pl.multiple_of(col * half, 16), half)
    own_norm = norm(points[mine, :], other_points[...])
    own_ids = lax.broadcasted_iota(jnp.int32, (half, size), 0) + (me * here + col * half)
    same = lax.broadcasted_iota(jnp.int32, (size, size), 0) == lax.broadcasted_iota(jnp.int32, (size, size), 1)
    eye = jnp.where(same, 1.0, 0.0)

    for i in range(here // size):
        levels[i * size:(i + 1) * size, :] = turned(weights[i:i + 1, :])

    whole_sum(0)
    for q in range(2, panels):
        between(q)
    forward(0)
    whole_sum(1)

    runs = gp.shape[1]
    lines = gp.shape[3]
    width = own_cols.shape[1]

    def gram_a(k, d):
        p = (place + d) % inner
        return remote(gp.at[k, :, p], ga.at[k, d - 1], ga_send.at[k, d - 1], ga_recv.at[k, d - 1],
                      layer * inner + p, col)

    def gram_b(k, i):
        target = k * runs + i
        slot = (layer - target + 2 * outer - 1) % outer
        return remote(gmid.at[k, i], gb.at[slot], gb_send.at[k, i], gb_recv.at[slot], target * inner + place, col)

    def gram_got(d):
        return remote(gmid.at[0, 0], gb.at[d - 1], gb_send.at[0, 0], gb_recv.at[d - 1],
                      ((layer + d) % outer) * inner + place, col)

    cut = outer - runs
    count = panels * size

    def half_rows(which):
        return pl.ds(pl.multiple_of(which * half, 16), half)

    def slot_of(z):
        return (layer - z + 2 * outer - 1) % outer

    def new_a(late, d):
        p = (place + d) % inner
        rows_of = slice(cut, outer) if late else slice(0, cut)
        return remote(nw.at[rows_of, p], na.at[d - 1, rows_of], na_send.at[late, d - 1], na_recv.at[late, d - 1],
                      layer * inner + p, col)

    def new_b(z):
        return remote(nmid.at[z], nb.at[slot_of(z)], nb_send.at[z], nb_recv.at[slot_of(z)], z * inner + place, col)

    def new_got(d):
        return remote(nmid.at[0], nb.at[d - 1], nb_send.at[0], nb_recv.at[d - 1],
                      ((layer + d) % outer) * inner + place, col)

    def side_a(d):
        p = (place + d) % inner
        return remote(cw.at[:, p], ca.at[d - 1], ca_send.at[d - 1], ca_recv.at[d - 1], layer * inner + p, col)

    def side_b(z):
        return remote(cmid.at[z], cb.at[slot_of(z)], cb_send.at[z], cb_recv.at[slot_of(z)], z * inner + place, col)

    def side_got(d):
        return remote(cmid.at[0], cb.at[d - 1], cb_send.at[0], cb_recv.at[d - 1],
                      ((layer + d) % outer) * inner + place, col)

    def new_early():
        for source, which in ((out_ref, col), (other_ref, 1 - col)):
            own_cols[half_rows(which), :width - size] = source[:, pl.ds(pl.multiple_of(col * width, 128), width - size)]

        @pl.when(col == 0)
        def _():
            for source, which in ((out_ref, col), (other_ref, 1 - col)):
                own_cols[half_rows(which), width - size:] = source[:, width - size:width]

        @pl.when(col == 1)
        def _():
            own_cols[:, width - size:] = jnp.zeros((here, size), bf16)

        block = jnp.dot(level_t[:count - size, :], own_cols[...], preferred_element_type=f32) * scale_by
        nw[:cut] = block.reshape(cut, inner, lines, width).astype(bf16)

    def new_sum(late):
        rows_of = slice(cut, outer) if late else slice(0, cut)
        total = nw[rows_of, place].astype(f32)
        for d in range(1, inner):
            new_a(late, d).wait_recv()
            total = total + na[d - 1, rows_of].astype(f32)
        nacc[rows_of] = total
        nmid[rows_of] = total.astype(bf16)
        for z in range(outer)[rows_of]:
            @pl.when(layer != z)
            def _():
                new_b(z).start()

    def gram_block(k):
        lanes = slice(k * size, (k + 1) * size)

        def part_of(source, which):
            for i in range(half // size):
                first = pl.multiple_of(which * half + i * size, size)
                block = source[i * size:(i + 1) * size, lanes].astype(f32) * levels[pl.ds(first, size), :]
                level_t[lanes, pl.ds(first, size)] = jnp.transpose(block).astype(bf16)
            spots = pl.ds(pl.multiple_of(which * half, size), half)
            return jnp.dot(level_t[lanes, spots], factor[half_rows(which), :], preferred_element_type=f32)

        block = part_of(out_ref, col)
        swap_panel(k).wait_recv()
        block = (block + part_of(other_ref, 1 - col)) * scale_by
        gp[k] = block.reshape(runs, inner, lines, factor.shape[1]).astype(bf16)

    def gram_send(k):
        for d in range(1, inner):
            gram_a(k, d).start()

    def gram_sum(k):
        total = gp[k, :, place].astype(f32)
        for d in range(1, inner):
            gram_a(k, d).wait_recv()
            total = total + ga[k, d - 1].astype(f32)
        gacc[k] = total
        gmid[k] = total.astype(bf16)
        for i in range(runs):
            @pl.when(layer != k * runs + i)
            def _():
                gram_b(k, i).start()

    def span(q):
        return slice(q * size, (q + 1) * size)

    def entries(xs, xo, ys, yo, q, row_norms):
        ts, to = piv[col, span(q), :], piv[1 - col, span(q), :]
        cross = dot(xs, ts[:, :fw]) + dot(xo, to[:, :fw])
        schur = dot(ys, ts[:, fw:]) + dot(yo, to[:, fw:])
        return jnp.exp(-(row_norms + norms[q, 0:1, :] - 2.0 * cross) / feats) + schur / (3.0 * rank)

    def less(value, x, y, count):
        if count:
            return value - dot(x[:, :count * size], y[:, :count * size])
        return value

    def head(r):
        ps, po = piv[col, span(r), :], piv[1 - col, span(r), :]
        pnorm = norm(ps[:, :fw], po[:, :fw])
        norms[r] = jnp.transpose(jnp.broadcast_to(pnorm, (size, size)))

        def against(k):
            return entries(ps[:, :fw], po[:, :fw], ps[:, fw:], po[:, fw:], k, pnorm)

        for k in range(r):
            m = less(against(k), prow[r], prow[k], k)
            if k < r - 1:
                prow[r, :, span(k)] = exact(m, inv[k]).astype(bf16)
            else:
                ready[...] = m
        early[...] = less(against(r) + RIDGE_LEVEL * eye, prow[r], prow[r], max(r - 1, 0))

    def begin(r):
        if r:
            fresh = exact(ready[...], inv[r - 1]).astype(bf16)
            prow[r, :, span(r - 1)] = fresh
            inv[r] = early[...] - dot(fresh, fresh)
        else:
            inv[r] = early[...]

    def solve(r):
        out_ref[:, span(r)] = exact(columns[...], inv[r]).astype(bf16)

    def fill(r, place_of):
        ids = owners[r:r + 1, :] * here + slots[r:r + 1, :]
        blocks = half // size
        for i in [i for i in range(blocks) if PLACES[i * len(PLACES) // blocks] == place_of]:
            own = pl.ds(pl.multiple_of(col * half + i * size, 16), size)
            value = entries(points[own, :], other_points[span(i), :], factor[own, :], other_factor[span(i), :], r,
                            own_norm[span(i), :])
            value = value + jnp.where(own_ids[span(i), :] == ids, RIDGE_LEVEL, 0.0)
            columns[span(i), :] = less(value, out_ref.at[span(i)], prow[r], r)

    arrive(0)
    head(0)
    for q in range(panels):
        def hook_a():
            if q > 0:
                swap_panel(q - 1).start()
            if q == 0:
                whole_sum(2)
            if q == 1:
                forward(2)
            fill(q, 1)

        def hook_b():
            if q > 0:
                gram_block(q - 1)
            if q == panels - 1:
                new_early()
            fill(q, 2)

        def hook_c():
            if q == 0:
                forward(1)
                whole_sum(3)
            elif q + 1 < panels:
                arrive(q + 1)
                head(q + 1)
            fill(q, 3)

        def hook_d():
            if q > 0:
                gram_send(q - 1)
            if q == panels - 1:
                for d in range(1, inner):
                    new_a(0, d).start()
            if q == 1:
                forward(3)
            fill(q, 4)

        def hook_e():
            if q == 0:
                arrive(1)
                head(1)
            if q > 1:
                gram_sum(q - 2)

        begin(q)
        if q:
            solve(q - 1)
        fill(q, 0)
        hooks = dict(zip((at * size // 16 for at in HOOKS), (hook_a, hook_b, hook_c, hook_d, hook_e)))
        factor_block(size, inv.at[q], rows, wide, hooks)
    solve(panels - 1)
    swap_panel(panels - 1).start()
    gram_block(panels - 1)
    gram_send(panels - 1)

    @pl.when(col == 1)
    def _():
        for source, which in ((out_ref, col), (other_ref, 1 - col)):
            own_cols[half_rows(which), width - size:] = source[:, count - size:]

    block = jnp.dot(level_t[count - size:, :], own_cols[...], preferred_element_type=f32) * scale_by
    nw[cut:] = block.reshape(outer - cut, inner, lines, width).astype(bf16)
    for d in range(1, inner):
        new_a(1, d).start()

    @pl.when(col == 1)
    def _():
        block = jnp.dot(level_t[:count - size, :], own_cols[:, width - size:], preferred_element_type=f32) * scale_by
        cw[...] = block.reshape(cut, inner, lines, size).astype(bf16)
        for d in range(1, inner):
            side_a(d).start()

    gram_sum(panels - 2)
    new_sum(0)
    gram_sum(panels - 1)
    new_sum(1)

    @pl.when(col == 1)
    def _():
        total = cw[:, place].astype(f32)
        for d in range(1, inner):
            side_a(d).wait_recv()
            total = total + ca[d - 1].astype(f32)
        cacc[...] = total
        cmid[...] = total.astype(bf16)
        for z in range(cut):
            @pl.when(layer != z)
            def _():
                side_b(z).start()

    total = gacc[layer // runs, layer % runs]
    for d in range(1, outer):
        gram_got(d).wait_recv()
        total = total + gb[d - 1].astype(f32)
    gram_old[...] = total
    total = nacc[layer]
    for d in range(1, outer):
        new_got(d).wait_recv()
        total = total + nb[d - 1].astype(f32)
    gram_new[...] = total

    @pl.when((col == 1) & (layer < cut))
    def _():
        total = gram_new[:, width - size:] + cacc[jnp.minimum(layer, cut - 1)]
        for d in range(1, outer):
            side_got(d).wait_recv()
            total = total + cb[d - 1].astype(f32)
        gram_new[:, width - size:] = total

    for d in range(1, inner):
        new_a(0, d).wait_send()
        new_a(1, d).wait_send()
    for z in range(outer):
        @pl.when(layer != z)
        def _():
            new_b(z).wait_send()

    @pl.when(col == 1)
    def _():
        for d in range(1, inner):
            side_a(d).wait_send()
        for z in range(cut):
            @pl.when(layer != z)
            def _():
                side_b(z).wait_send()

    for c in swap:
        c.wait_send()
    for q in range(panels):
        swap_panel(q).wait_send()
        for d in range(1, inner):
            within(q, d).wait_send()
            gram_a(q, d).wait_send()
        for i in range(runs):
            @pl.when(layer != q * runs + i)
            def _():
                gram_b(q, i).wait_send()
        for c in sends_b(q):
            c.wait_send()
        for d in range(1, inner):
            around(q, d).wait_send()
        for d in range(inner):
            across(q, d).wait_send()


def write_kernel(a, b, c, x, y, z, sems):
    copies = [pltpu.make_async_copy(s, d, sems.at[i]) for i, (s, d) in enumerate(((a, x), (b, y), (c, z)))]
    for c in copies:
        c.start()
    for c in copies:
        c.wait()


def body(points, factor, weights, pivot_slots, pivot_owners):
    here, fw = points.shape
    rank = factor.shape[1]
    panels, size = pivot_slots.shape
    rows = lax.axis_size("rows")
    count = panels * size
    chunk = count // rows
    width = fw + rank
    half = here // 2
    bf16, f32 = jnp.bfloat16, jnp.float32
    vm = pl.BlockSpec(memory_space=VMEM)
    hbm = pl.BlockSpec(memory_space=pl.ANY)
    sem = lambda *n: pltpu.SemaphoreType.DMA(n)
    limit = 60 * 1024 * 1024

    split = rows // panels if rows < panels * panels else panels
    layers = rows // split
    piece = size // split
    runs = layers // panels
    cut = layers - runs
    share = count // 2
    scale = size / math.sqrt(here * rows)
    outs = pl.pallas_call(
        functools.partial(panel_kernel, split, layers, scale),
        out_shape=(
            pltpu.VMEM((here, share), bf16), pltpu.VMEM((chunk, rank), f32), pltpu.VMEM((chunk, share), f32),
        ),
        in_specs=[vm, vm, hbm, hbm, vm], out_specs=(vm,) * 3, name="panels",
        scratch_shapes=[
            VMEM((half, count), bf16), VMEM((half, count), bf16), VMEM((count, here), bf16),
            VMEM((panels, runs, split, chunk, rank), bf16),
            VMEM((panels, split - 1, runs, chunk, rank), bf16),
            VMEM((panels, runs, chunk, rank), f32), VMEM((panels, runs, chunk, rank), bf16),
            VMEM((layers, chunk, rank), bf16),
            VMEM((layers, split, chunk, share), bf16),
            VMEM((split - 1, layers, chunk, share), bf16),
            VMEM((layers, chunk, share), f32), VMEM((layers, chunk, share), bf16),
            VMEM((layers - 1, chunk, share), bf16),
            VMEM((cut, split, chunk, size), bf16), VMEM((split - 1, cut, chunk, size), bf16),
            VMEM((cut, chunk, size), f32), VMEM((cut, chunk, size), bf16), VMEM((layers - 1, chunk, size), bf16),
            sem(panels, split - 1), sem(panels, split - 1), sem(panels, runs), sem(layers),
            sem(2, split - 1), sem(2, split - 1), sem(layers), sem(layers - 1),
            sem(split - 1), sem(split - 1), sem(cut), sem(layers - 1),
            VMEM((here, fw), bf16), VMEM((here, rank), bf16), sem(2),
            VMEM((count, width), bf16), VMEM((2, count, width), bf16),
            VMEM((half, fw), bf16), VMEM((half, rank), bf16),
            VMEM((panels, split - 1, piece, width), bf16),
            VMEM((panels, layers - 1, piece, width), bf16),
            VMEM((panels, piece, width), bf16), VMEM((panels, (layers - 1).bit_length(), piece, width), bf16),
            VMEM((panels, size, count), bf16),
            VMEM((panels, size, size), f32), VMEM((panels, size, size), f32),
            VMEM((size, size), f32), VMEM((size, size), f32), VMEM((half, size), f32),
            VMEM((here, size), f32),
            VMEM((4 * BLOCK, size), f32), VMEM((6 * BLOCK, BLOCK, size), f32),
            sem(panels, split - 1), sem(panels, split - 1), sem(panels, layers - 1), sem(panels, layers - 1),
            sem(panels), sem(panels), sem(panels, split - 1), sem(panels, split - 1),
            sem(panels, split), sem(panels, split), sem(2), sem(2),
        ],
        compiler_params=pltpu.CompilerParams(collective_id=0, has_side_effects=True, vmem_limit_bytes=limit),
    )(pivot_slots, pivot_owners, points, factor, weights.reshape(here // size, size))
    return pl.pallas_call(
        write_kernel,
        out_shape=(
            jax.ShapeDtypeStruct((here, share), bf16),
            jax.ShapeDtypeStruct((chunk, rank), f32),
            jax.ShapeDtypeStruct((chunk, share), f32),
        ),
        in_specs=[vm] * 3, out_specs=(hbm,) * 3, name="write",
        scratch_shapes=[sem(3)],
    )(*[pltpu.with_memory_space_constraint(v, pltpu.VMEM) for v in outs])


def solution(mesh):
    return jax.shard_map(
        body,
        mesh=mesh,
        in_specs=(P("rows", "cols"), P("rows", "cols"), P("rows"), P(), P()),
        out_specs=(P("rows", "cols"), P("rows", "cols"), P("rows", "cols")),
        check_vma=False,
    )
```
